32 devices in a mesh: mem: 4 (over y, x), lat: 4 (over z), win: 2 (over core).
Axes of the slice: x: 2, y: 2, z: 4, core: 2. Of those that a mesh axis runs over, the one named last changes fastest.
Arguments:
- ensemble: float32 [8, 8, 32, 512], P('mem', None, 'lat'), may hold values from -6 to 6
- weights: float32 [2, 8, 32, 512], P('win', 'mem', 'lat'), may hold values from -6 to 6
- diffusivity: float32 [8, 32, 512], P(None, 'lat', 'mem'), may hold values from 0.05 to 0.4
- coupling: float32 [8, 8], replicated, may hold values from -0.5 to 0.5
- tl_steps: int32 [2], P('win'), may hold values from 1 to 6
- obs_cell: int32 [16384], P(('mem', 'lat')), may hold values from 0 to 8191
- obs_window: int32 [16384], P(('mem', 'lat')), may hold values from 0 to 1
- obs_value: float32 [16384], P(('mem', 'lat')), may hold values from -6 to 6
- obs_weight: float32 [16384], P(('mem', 'lat')), may hold values from 1 to 8
- error_weight: float32 [8], replicated, may hold values from 0.5 to 4
Outputs:
- control: float32 [2, 8, 32, 512], P('win', 'mem', 'lat')
- increment: float32 [2, 8, 32, 512], P('win', None, 'lat', 'mem')
The draws below stay inside these ranges and needn't reach their ends.
Inputs may be any that keep to these rules, and one draw needn't show every extreme that they name: `tl_steps`: how many of the 6 tangent steps the subwindow takes. `obs_cell`: index of the observed cell in the block of 8 x 8 x 128 cells that the observation's device holds (mem index, lat index), flattened as variable, row, longitude.
All inputs are finite; a program needn't handle non-finite values.
Results may differ from the reference program's by a relative error of at most 0.00015.
Values sent between devices are 32-bit elements; how exact they have to be, the bound alone decides.
No kernel may reach another device: no remote copies, remote signals or barrier semaphores. Data moves between devices by JAX's collectives and lax.ppermute only.
A program may use at most 64 MiB of HBM per device.

```python
import math
import jax
import jax.numpy as jnp
from jax import lax

NV = 8
LB = 8
LON_DEV = 128
OBS_DEV = 1024
KMAX = 6
DIFF = 2
ITERS = 2
M = 8
NLAT = 32
NLON = 512
NWIN = 2
NOBS = 16384
N_MEM = 4
N_LAT = 4
N_WIN = 2


def touch_ends(array, own_key, smallest, high):
    index_at = [jax.random.randint(jax.random.fold_in(own_key, axis), (), 0, length) for axis, length in enumerate(array.shape)]
    longest = array.shape.index(max(array.shape))
    beside = index_at[:longest] + [(index_at[longest] + 1) % array.shape[longest]] + index_at[longest + 1:]
    return array.at[tuple(index_at)].set(smallest).at[tuple(beside)].set(high)


def shard_levels(key, extent, shards, low, top_value):
    gain, own = 1.0, jax.random.fold_in(key, 6)
    for position, parts in shards:
        steps = jnp.exp(jax.random.uniform(jax.random.fold_in(own, position), (parts,), jnp.float32, low / len(shards), top_value / len(shards)))
        gain = gain * jnp.repeat(steps, extent[position] // parts).reshape([-1 if axis == position else 1 for axis in range(len(extent))])
    return gain


def scatter_about(key, dims, width, limit, split=(), held_as=jnp.bfloat16):
    array = jax.random.normal(key, dims, jnp.float32) * width
    if len(split) > 0:
        array = shard_levels(key, dims, split, -0.22, 0.18) * array
    return jnp.clip(array, min=-limit, max=limit).astype(held_as)


def setup_inputs(seed: int = 0) -> dict:
    keys = jax.random.split(jax.random.key(seed), 11)
    ensemble = scatter_about(keys[0], (M, NV, NLAT, NLON), 1.0, 6.0, ((0, 4), (2, 4)), jnp.float32)
    weights = scatter_about(keys[1], (NWIN, M, NLAT, NLON), 1.0, 6.0, ((0, 2), (1, 4), (2, 4)), jnp.float32)
    diffusivity = jnp.clip(jnp.exp(math.log(0.4) - 2.0794415 * jax.random.uniform(keys[2], (NV, NLAT, NLON), jnp.float32) ** shard_levels(keys[2], (NV, NLAT, NLON), ((1, 4), (2, 4)), -0.2, 0.2)), 0.05, 0.4)
    coupling = scatter_about(keys[3], (NV, NV), 0.1, 0.5, (), jnp.float32)
    tl_steps = jax.random.randint(keys[4], (NWIN,), 1, KMAX + 1).astype(jnp.int32)
    obs_cell = touch_ends(jax.random.randint(keys[5], (NOBS,), 0, NV * LB * LON_DEV), jax.random.fold_in(keys[5], 1), 0, (NV * LB * LON_DEV) - 1).astype(jnp.int32)
    obs_window = touch_ends(jax.random.randint(keys[6], (NOBS,), 0, NWIN), jax.random.fold_in(keys[6], 1), 0, NWIN - 1).astype(jnp.int32)
    obs_value = scatter_about(keys[7], (NOBS,), 1.0, 6.0, ((0, 16),), jnp.float32)
    obs_weight = jnp.clip(jnp.exp(math.log(8.0) - 2.0794415 * jax.random.uniform(keys[8], (NOBS,), jnp.float32) ** shard_levels(keys[8], (NOBS,), ((0, 16),), -0.2, 0.2)), 1.0, 8.0)
    error_weight = jnp.clip(jnp.exp(jax.random.uniform(keys[9], (NV,), jnp.float32, math.log(0.5), math.log(4.0))), 0.5, 4.0)
    return dict(ensemble=ensemble, weights=weights, diffusivity=diffusivity, coupling=coupling, tl_steps=tl_steps, obs_cell=obs_cell, obs_window=obs_window, obs_value=obs_value, obs_weight=obs_weight, error_weight=error_weight)


KAPPA = 0.125
DESCENT = 0.25
HIGHEST = lax.Precision.HIGHEST

def relax(padded):
    middle = padded[..., 1:-1, :]
    beside_all = padded[..., 2:, :] + padded[..., :-2, :] + jnp.roll(middle, 1, -1) + jnp.roll(middle, -1, -1)
    return middle + KAPPA * (beside_all - 4.0 * middle)

def diffuse(values):
    widths = [(0, 0)] * (values.ndim - 2) + [(1, 1), (0, 0)]
    for repeat in range(DIFF):
        values = relax(jnp.pad(values, widths))
    return values

def forward(state, diffusivity, coupling, tl_steps):
    for section_index in range(KMAX):
        padded = jnp.pad(state, ((0, 0), (0, 0), (1, 1), (0, 0)))
        second = padded[:, :, 2:] + padded[:, :, :-2] - 2.0 * state
        mixed = jnp.einsum('vu,wurl->wvrl', coupling, state, precision=HIGHEST)
        moved = state + diffusivity[None] * second + mixed
        state = jnp.where((section_index < tl_steps)[:, None, None, None], moved, state)
    return state

def backward(state, diffusivity, coupling, tl_steps):
    for section_index in reversed(range(KMAX)):
        weighted = diffusivity[None] * state
        padded = jnp.pad(weighted, ((0, 0), (0, 0), (1, 1), (0, 0)))
        second = padded[:, :, 2:] + padded[:, :, :-2] - 2.0 * weighted
        mixed = jnp.einsum('uv,wurl->wvrl', coupling, state, precision=HIGHEST)
        moved = state + second + mixed
        state = jnp.where((section_index < tl_steps)[:, None, None, None], moved, state)
    return state

def observe(ends, obs_cell, obs_window, obs_value, obs_weight):
    nblock = N_MEM * N_LAT
    blocks = ends.reshape(N_WIN, NV, N_LAT, LB, N_MEM, LON_DEV).transpose(0, 4, 2, 1, 3, 5).reshape(N_WIN, nblock, NV * LB * LON_DEV)
    cells = obs_cell.reshape(nblock, OBS_DEV)
    picked = jnp.take_along_axis(blocks, cells[None], axis=2)
    window_ids = jnp.arange(N_WIN, dtype=jnp.int32)
    chosen = obs_window.reshape(nblock, OBS_DEV)[None] == window_ids[:, None, None]
    innovation = jnp.where(chosen, (picked - obs_value.reshape(nblock, OBS_DEV)[None]) * obs_weight.reshape(nblock, OBS_DEV)[None], 0.0)
    block_rows = jnp.arange(nblock, dtype=jnp.int32)[:, None]
    spread = jnp.zeros_like(blocks).at[:, block_rows, cells].add(innovation)
    return spread.reshape(N_WIN, N_MEM, N_LAT, NV, LB, LON_DEV).transpose(0, 3, 2, 4, 1, 5).reshape(N_WIN, NV, NLAT, NLON)

def reference(ensemble, weights, diffusivity, coupling, tl_steps, obs_cell, obs_window, obs_value, obs_weight, error_weight):
    member_scale = 1.0 / math.sqrt(M - 1)
    control = weights
    has_before = (jnp.arange(N_WIN) > 0)[:, None, None, None]
    increment = None
    for iteration in range(ITERS):
        smoothed = diffuse(control)
        increment = jnp.einsum('mvrl,wmrl->wvrl', ensemble, smoothed, precision=HIGHEST) * member_scale
        ends = forward(increment, diffusivity, coupling, tl_steps)
        previous = jnp.concatenate([jnp.zeros_like(ends[:1]), ends[:-1]], 0)
        misfit = jnp.where(has_before, error_weight[None, :, None, None] * (previous - increment), 0.0)
        misfit_next = jnp.concatenate([misfit[1:], jnp.zeros_like(misfit[:1])], 0)
        observed = observe(ends, obs_cell, obs_window, obs_value, obs_weight)
        gradient = backward(observed + misfit_next, diffusivity, coupling, tl_steps) - misfit
        back_members = jnp.einsum('mvrl,wvrl->wmrl', ensemble, gradient, precision=HIGHEST) * member_scale
        control = control - DESCENT * (control + diffuse(back_members))
    return (control, increment)
```

```python
import math

import jax
import jax.numpy as jnp
from jax import lax
from jax.experimental import pallas as pl
from jax.experimental.pallas import tpu as pltpu
from jax.sharding import PartitionSpec as P

KMAX = 6
DIFF = 2
ITERS = 2
KAPPA = 0.125
DESCENT = 0.25

ROWS = 8
LANES = 128
SPAN = 32
GROUPS = LANES // SPAN


def roll(x, shift, axis):
    shift %= x.shape[axis]
    return x if shift == 0 else pltpu.roll(x, shift, axis)


def lane_ids():
    return lax.broadcasted_iota(jnp.int32, (ROWS, LANES), 1)


def pad4(units):
    return list(units) + [jnp.zeros_like(units[0])] * (GROUPS - len(units))


def exchange4(x):
    group = lane_ids() // SPAN
    low, even = group < 2, group % 2 == 0
    a = [jnp.where(low, x[u], roll(x[u + 2], 64, 1)) for u in range(2)]
    b = [jnp.where(low, roll(x[u], 64, 1), x[u + 2]) for u in range(2)]
    out = []
    for first, second in (a, b):
        out.append(jnp.where(even, first, roll(second, SPAN, 1)))
        out.append(jnp.where(even, roll(first, -SPAN, 1), second))
    return out


def windows(units, own):
    halo, phases, length = (SPAN - own) // 2, SPAN // own, units[0].shape[1]
    for phase in range(phases):
        moved = pad4([roll(u, halo - own * phase, 1) for u in units])
        for tile in range(length // LANES):
            parts = exchange4([m[:, tile * LANES : (tile + 1) * LANES] for m in moved])
            for q, part in enumerate(parts):
                yield (tile * GROUPS + q) * phases + phase, part


class Sizes:
    def __init__(self, mesh_shape, members_here, variables, lon, obs_here):
        self.mem, self.lat, self.win = (mesh_shape[a] for a in ("mem", "lat", "win"))
        self.devices = self.mem * self.lat * self.win
        self.members_here, self.variables, self.lon = members_here, variables, lon
        self.members = members_here * self.mem
        self.vars_here = variables // self.win
        self.own = lon // self.devices
        self.halo = (SPAN - self.own) // 2
        self.tiles = self.lat // 2
        self.pairs = self.win // 2
        self.obs_rows = obs_here // self.win // LANES
        self.ens_regs = pl.cdiv(members_here * self.vars_here, GROUPS)
        self.dif_regs = pl.cdiv(self.vars_here, GROUPS)
        self.obs_regs = pl.cdiv(4 * self.obs_rows, ROWS)
        self.dif_at = ROWS * self.ens_regs
        self.wts_at = self.dif_at + ROWS * self.dif_regs
        self.obs_at = self.wts_at + ROWS
        self.chunk = self.obs_at + ROWS * self.obs_regs
        assert lon // self.mem == LANES and members_here < GROUPS
        assert self.halo >= 2 * DIFF * ITERS
        assert self.lat % 2 == 0 and self.win % 2 == 0 and variables % self.win == 0
        assert SPAN % self.own == 0 and variables * self.own <= LANES
        assert obs_here % (self.win * LANES) == 0


def pack_kernel(z, steps, ens, wts, dif, cell, window, value, weight, out, obs):
    k = lax.axis_index("win")
    units = [ens[m, k * z.vars_here + v] for m in range(z.members_here) for v in range(z.vars_here)]
    for reg in range(z.ens_regs):
        for d, part in windows(units[reg * GROUPS : (reg + 1) * GROUPS], z.own):
            out[d, reg * ROWS : (reg + 1) * ROWS, :] = part
    per_block = LANES // z.own
    for reg in range(z.dif_regs):
        mine = range(reg * GROUPS, min(z.vars_here, (reg + 1) * GROUPS))
        at = z.dif_at + reg * ROWS
        for d, part in windows([dif[k * z.vars_here + v] for v in mine], z.own):
            for block in range(z.mem):
                out[block * per_block + d, at : at + ROWS, :] = part
    count = jnp.full((ROWS, LANES), steps[0], jnp.int32).astype(jnp.float32)
    holds_weights = lane_ids() // SPAN < z.members_here
    for d, part in windows([wts[0, m] for m in range(z.members_here)], z.own):
        out[d, z.wts_at : z.wts_at + ROWS, :] = jnp.where(holds_weights, part, count)
    n = z.obs_rows
    for a, ref in enumerate((cell, window, value, weight)):
        rows = ref[0:n, :]
        for other in range(1, z.win):
            rows = jnp.where(k == other, ref[other * n : (other + 1) * n, :], rows)
        obs[a * n : (a + 1) * n, :] = rows.astype(jnp.float32)
    table = obs[...]
    for d in range(z.devices):
        out[d, z.obs_at :, :] = table


def spread4(first, second):
    group = lane_ids() // SPAN
    low, even = group < 2, group % 2 == 0
    a = jnp.where(even, first, roll(second, SPAN, 1))
    b = jnp.where(even, roll(first, -SPAN, 1), second)
    a2, b2 = roll(a, 64, 1), roll(b, 64, 1)
    return [jnp.where(low, a, a2), jnp.where(low, b, b2), jnp.where(low, a2, a), jnp.where(low, b2, b)]


def place(pieces, width):
    target = lane_ids() // width
    out = None
    for g, (x, lane) in enumerate(pieces):
        moved = roll(x, width * g - lane, 1)
        out = moved if out is None else jnp.where(target == g, moved, out)
    return out


def split3(x):
    high = x.astype(jnp.bfloat16).astype(jnp.float32)
    middle = (x - high).astype(jnp.bfloat16).astype(jnp.float32)
    return high, middle, x - high - middle


def descend_kernel(z, scale, coup, error_weight, recv, out, ens, dif, slope, bias):
    i, j, k = (lax.axis_index(a) for a in ("mem", "lat", "win"))
    d = (i * z.lat + j) * z.win + k
    start = lax.rem(d * z.own - z.halo + z.lon, z.lon)
    left = lax.div(start, LANES)
    right = lax.div(lax.rem(start + SPAN - 1, z.lon), LANES)
    lanes = lane_ids()
    sub = lax.broadcasted_iota(jnp.int32, (ROWS, LANES), 0)
    group = lanes // SPAN
    upper = group % 2 == 0
    in_left = start + lanes % SPAN < (left + 1) * LANES
    T, NV, M = z.tiles, z.variables, z.members

    def source(mem, lat, win):
        return (mem * z.lat + lat) * z.win + win

    for mem in range(z.mem):
        for win in range(z.win):
            for reg in range(z.ens_regs):
                for t in range(T):
                    got = spread4(*(recv[source(mem, h * T + t, win), reg * ROWS : (reg + 1) * ROWS, :] for h in range(2)))
                    for u, part in enumerate(got):
                        unit = reg * GROUPS + u
                        if unit < z.members_here * z.vars_here:
                            m = mem * z.members_here + unit // z.vars_here
                            v = win * z.vars_here + unit % z.vars_here
                            ens[m, v, t] = part
    for win in range(z.win):
        for reg in range(z.dif_regs):
            rows = pl.ds(z.dif_at + reg * ROWS, ROWS)
            for t in range(T):
                both = [
                    jnp.where(in_left, recv[source(left, h * T + t, win), rows, :], recv[source(right, h * T + t, win), rows, :])
                    for h in range(2)
                ]
                for u, part in enumerate(spread4(*both)):
                    if reg * GROUPS + u < z.vars_here:
                        dif[win * z.vars_here + reg * GROUPS + u, t] = part

    def weights_of(mem, lat, win):
        return recv[source(mem, lat, win), z.wts_at : z.wts_at + ROWS, :]

    control = []
    for m in range(M):
        mem, unit = divmod(m, z.members_here)
        control.append([
            [
                place([(weights_of(mem, h * T + t, 2 * p + w), SPAN * unit) for w in range(2) for h in range(2)], SPAN)
                for t in range(T)
            ]
            for p in range(z.pairs)
        ])
    counts = [
        place([(weights_of(0, 0, 2 * p + w), SPAN * z.members_here) for w in range(2) for h in range(2)], SPAN).astype(jnp.int32)
        for p in range(z.pairs)
    ]

    row_id = lax.broadcasted_iota(jnp.int32, (NV * ROWS, LANES), 0)
    key_id = lax.broadcasted_iota(jnp.int32, (z.win * SPAN, LANES), 0)
    n = z.obs_rows
    for lat in range(z.lat):
        rows_hot, parts = [], [[] for _ in range(3)]
        for side, block in enumerate((left, right)):
            for win in range(z.win):
                table = recv[source(block, lat, win), z.obs_at :, :]
                where = table[0:n, :].astype(jnp.int32)
                weight = table[3 * n : 4 * n, :]
                weighted = weight * table[2 * n : 3 * n, :]
                lane = block * LANES + where % LANES - start
                lane = jnp.where(lane < 0, lane + z.lon, lane)
                inside = lane < SPAN
                if side == 1:
                    inside &= left != right
                key = jnp.where(inside, table[n : 2 * n, :].astype(jnp.int32) * SPAN + lane, -1)
                row = where // LANES
                splits = list(zip(split3(weight), split3(weighted)))
                for x in range(n):
                    one = slice(x, x + 1)
                    hit = jnp.broadcast_to(key[one], key_id.shape) == key_id
                    rows_hot.append(jnp.where(jnp.broadcast_to(row[one], row_id.shape) == row_id, 1.0, 0.0).astype(jnp.bfloat16))
                    for part, pair in zip(parts, splits):
                        part.append(
                            jnp.concatenate(
                                [jnp.where(hit, jnp.broadcast_to(y[one], hit.shape), 0.0).astype(jnp.bfloat16) for y in pair], 0
                            )
                        )
        hot = jnp.concatenate(rows_hot, 1)
        total = 0.0
        for part in reversed(parts):
            total += lax.dot_general(
                hot, jnp.concatenate(part, 1), (((1,), (1,)), ((), ())), preferred_element_type=jnp.float32
            )
        h, t = divmod(lat, T)
        for q, field in enumerate((slope, bias)):
            for p in range(z.pairs):
                for w in range(2):
                    lane = (q * z.win + 2 * p + w) * SPAN
                    tile, at = divmod(lane, LANES)
                    mine = group == 2 * w + h
                    for v in range(NV):
                        x = total[v * ROWS : (v + 1) * ROWS, tile * LANES : (tile + 1) * LANES]
                        x = roll(x, SPAN * (2 * w + h) - at, 1)
                        if w == 0 and h == 0:
                            field[p, v, t] = x
                        else:
                            field[p, v, t] = jnp.where(mine, x, field[p, v, t])

    first, last = sub == 0, sub == ROWS - 1

    def beside(x):
        down = [roll(a, 1, 0) for a in x]
        up = [roll(a, -1, 0) for a in x]
        before_first = jnp.where(upper, 0.0, roll(down[T - 1], SPAN, 1))
        after_last = jnp.where(upper, roll(up[0], -SPAN, 1), 0.0)
        return [
            jnp.where(first, down[t - 1] if t else before_first, down[t])
            + jnp.where(last, up[t + 1] if t < T - 1 else after_last, up[t])
            for t in range(T)
        ]

    def smooth(x):
        for _ in range(DIFF):
            x = [
                a + KAPPA * (rows + roll(a, 1, 1) + roll(a, -1, 1) - 4.0 * a)
                for a, rows in zip(x, beside(x))
            ]
        return x

    def weigh(terms):
        total = None
        for factor, x in terms:
            total = factor * x if total is None else total + factor * x
        return total

    def forward(state, p, most):
        def step(section, flat):
            u = [list(flat[v * T : (v + 1) * T]) for v in range(NV)]
            on = section < counts[p]
            moved = []
            for v in range(NV):
                near = beside(u[v])
                for t in range(T):
                    x = u[v][t]
                    y = x + dif[v, t] * (near[t] - 2.0 * x) + weigh((coup[v, w], u[w][t]) for w in range(NV))
                    moved.append(jnp.where(on, y, x))
            return tuple(moved)

        flat = lax.fori_loop(0, most, step, tuple(x for v in state for x in v))
        return [list(flat[v * T : (v + 1) * T]) for v in range(NV)]

    def backward(state, p, most):
        def step(section, flat):
            u = [list(flat[v * T : (v + 1) * T]) for v in range(NV)]
            on = section < counts[p]
            moved = []
            for v in range(NV):
                weighted = [dif[v, t] * u[v][t] for t in range(T)]
                near = beside(weighted)
                for t in range(T):
                    x = u[v][t]
                    y = x + (near[t] - 2.0 * weighted[t]) + weigh((coup[w, v], u[w][t]) for w in range(NV))
                    moved.append(jnp.where(on, y, x))
            return tuple(moved)

        flat = lax.fori_loop(0, most, step, tuple(x for v in state for x in v))
        return [list(flat[v * T : (v + 1) * T]) for v in range(NV)]

    most = [jnp.max(c) for c in counts]
    later = group >= 2
    zero = jnp.zeros((ROWS, LANES), jnp.float32)
    for _ in range(ITERS):
        increment, ends = [], []
        smoothed = [[smooth(control[m][p]) for p in range(z.pairs)] for m in range(M)]
        for p in range(z.pairs):
            increment.append(
                [[weigh((ens[m, v, t], smoothed[m][p][t]) for m in range(M)) * scale for t in range(T)] for v in range(NV)]
            )
            ends.append(forward(increment[p], p, most[p]))
        misfit = []
        for p in range(z.pairs):
            misfit.append([])
            for v in range(NV):
                misfit[p].append([])
                for t in range(T):
                    before = roll(ends[p][v][t], 64, 1)
                    if p:
                        before = jnp.where(later, before, roll(ends[p - 1][v][t], 64, 1))
                    x = error_weight[v] * (before - increment[p][v][t])
                    misfit[p][v].append(x if p else jnp.where(later, x, 0.0))
        members_back = [[] for _ in range(M)]
        for p in range(z.pairs):
            forcing = []
            for v in range(NV):
                forcing.append([])
                for t in range(T):
                    after = roll(misfit[p + 1][v][t], 64, 1) if p + 1 < z.pairs else zero
                    after = jnp.where(later, after, roll(misfit[p][v][t], 64, 1))
                    forcing[v].append(slope[p, v, t] * ends[p][v][t] - bias[p, v, t] + after)
            adjoint = backward(forcing, p, most[p])
            gradient = [[adjoint[v][t] - misfit[p][v][t] for t in range(T)] for v in range(NV)]
            for m in range(M):
                members_back[m].append(
                    [weigh((ens[m, v, t], gradient[v][t]) for v in range(NV)) * scale for t in range(T)]
                )
        for m in range(M):
            for p in range(z.pairs):
                pulled = smooth(members_back[m][p])
                control[m][p] = [c - DESCENT * (c + x) for c, x in zip(control[m][p], pulled)]

    for lat in range(z.lat):
        h, t = divmod(lat, T)
        for win in range(z.win):
            p, w = divmod(win, 2)
            lane = SPAN * (2 * w + h) + z.halo
            grown = place([(increment[p][v][t], lane) for v in range(NV)], z.own)
            for mem in range(z.mem):
                to = source(mem, lat, win)
                mine = [control[mem * z.members_here + m][p][t] for m in range(z.members_here)]
                out[to, 0:ROWS, :] = place([(x, lane) for x in mine], z.own)
                out[to, ROWS : 2 * ROWS, :] = grown


def unpack_kernel(z, recv, control, increment):
    per_tile = LANES // z.own
    for m in range(z.members_here):
        for tile in range(z.lon // LANES):
            control[0, m, :, tile * LANES : (tile + 1) * LANES] = place(
                [(recv[tile * per_tile + q, 0:ROWS, :], z.own * m) for q in range(per_tile)], z.own
            )
    i = lax.axis_index("mem")
    for v in range(z.variables):
        increment[0, v] = place(
            [(recv[i * per_tile + q, ROWS : 2 * ROWS, :], z.own * v) for q in range(per_tile)], z.own
        )


def solution(mesh):
    smem = pl.BlockSpec(memory_space=pltpu.SMEM)
    vmem = pl.BlockSpec(memory_space=pltpu.VMEM)
    f32 = jnp.float32

    def local(ensemble, weights, diffusivity, coupling, tl_steps, obs_cell, obs_window, obs_value, obs_weight, error_weight):
        z = Sizes(mesh.shape, ensemble.shape[0], ensemble.shape[1], ensemble.shape[3], obs_cell.shape[0])
        scale = 1.0 / math.sqrt(z.members - 1)
        axes = ("mem", "lat", "win")
        tables = [x.reshape(-1, LANES) for x in (obs_cell, obs_window, obs_value, obs_weight)]
        sent = pl.pallas_call(
            lambda *refs: pack_kernel(z, *refs),
            out_shape=jax.ShapeDtypeStruct((z.devices, z.chunk, LANES), f32),
            in_specs=[smem] + [vmem] * 7,
            out_specs=vmem,
            scratch_shapes=[pltpu.VMEM((ROWS * z.obs_regs, LANES), f32)],
            name="pack",
        )(tl_steps, ensemble, weights, diffusivity, *tables)
        got = lax.all_to_all(sent, axes, 0, 0)
        field = pltpu.VMEM((z.pairs, z.variables, z.tiles, ROWS, LANES), f32)
        back = pl.pallas_call(
            lambda *refs: descend_kernel(z, scale, *refs),
            out_shape=jax.ShapeDtypeStruct((z.devices, 2 * ROWS, LANES), f32),
            in_specs=[smem, smem, vmem],
            out_specs=vmem,
            scratch_shapes=[
                pltpu.VMEM((z.members, z.variables, z.tiles, ROWS, LANES), f32),
                pltpu.VMEM((z.variables, z.tiles, ROWS, LANES), f32),
                field,
                field,
            ],
            name="descend",
        )(coupling, error_weight, got)
        home = lax.all_to_all(back, axes, 0, 0)
        return pl.pallas_call(
            lambda *refs: unpack_kernel(z, *refs),
            out_shape=(
                jax.ShapeDtypeStruct(weights.shape, f32),
                jax.ShapeDtypeStruct((1, z.variables, ROWS, LANES), f32),
            ),
            in_specs=[vmem],
            out_specs=(vmem, vmem),
            name="unpack",
        )(home)

    return jax.shard_map(
        local,
        mesh=mesh,
        in_specs=(
            P("mem", None, "lat", None),
            P("win", "mem", "lat", None),
            P(None, "lat", "mem"),
            P(),
            P("win"),
            P(("mem", "lat")),
            P(("mem", "lat")),
            P(("mem", "lat")),
            P(("mem", "lat")),
            P(),
        ),
        out_specs=(P("win", "mem", "lat", None), P("win", None, "lat", "mem")),
        check_vma=False,
    )
```

```python
import math

import jax
import jax.numpy as jnp
from jax import lax
from jax.experimental import pallas as pl
from jax.experimental.pallas import tpu as pltpu
from jax.sharding import PartitionSpec as P

KMAX = 6
DIFF = 2
ITERS = 2
KAPPA = 0.125
DESCENT = 0.25

ROWS = 8
LANES = 128
SPAN = 32
GROUPS = LANES // SPAN


def roll(x, shift, axis):
    shift %= x.shape[axis]
    return x if shift == 0 else pltpu.roll(x, shift, axis)


def lane_ids():
    return lax.broadcasted_iota(jnp.int32, (ROWS, LANES), 1)


def pad4(units):
    return list(units) + [jnp.zeros_like(units[0])] * (GROUPS - len(units))


def exchange4(x):
    group = lane_ids() // SPAN
    low, even = group < 2, group % 2 == 0
    a = [jnp.where(low, x[u], roll(x[u + 2], 64, 1)) for u in range(2)]
    b = [jnp.where(low, roll(x[u], 64, 1), x[u + 2]) for u in range(2)]
    out = []
    for first, second in (a, b):
        out.append(jnp.where(even, first, roll(second, SPAN, 1)))
        out.append(jnp.where(even, roll(first, -SPAN, 1), second))
    return out


def windows(units, own):
    halo, phases, length = (SPAN - own) // 2, SPAN // own, units[0].shape[1]
    for phase in range(phases):
        moved = pad4([roll(u, halo - own * phase, 1) for u in units])
        for tile in range(length // LANES):
            parts = exchange4([m[:, tile * LANES : (tile + 1) * LANES] for m in moved])
            for q, part in enumerate(parts):
                yield (tile * GROUPS + q) * phases + phase, part


class Sizes:
    def __init__(self, mesh_shape, members_here, variables, lon, obs_here):
        self.mem, self.lat, self.win = (mesh_shape[a] for a in ("mem", "lat", "win"))
        self.devices = self.mem * self.lat * self.win
        self.members_here, self.variables, self.lon = members_here, variables, lon
        self.members = members_here * self.mem
        self.vars_here = variables // self.win
        self.own = lon // self.devices
        self.halo = (SPAN - self.own) // 2
        self.tiles = self.lat // 2
        self.pairs = self.win // 2
        self.obs_rows = obs_here // self.win // LANES
        self.ens_regs = pl.cdiv(members_here * self.vars_here, GROUPS)
        self.dif_regs = pl.cdiv(self.vars_here, GROUPS)
        self.obs_regs = pl.cdiv(4 * self.obs_rows, ROWS)
        self.dif_at = ROWS * self.ens_regs
        self.wts_at = self.dif_at + ROWS * self.dif_regs
        self.obs_at = self.wts_at + ROWS
        self.chunk = self.obs_at + ROWS * self.obs_regs
        assert lon // self.mem == LANES and members_here < GROUPS
        assert self.halo >= 2 * DIFF * ITERS
        assert self.lat % 2 == 0 and self.win % 2 == 0 and variables % self.win == 0
        assert SPAN % self.own == 0 and variables * self.own <= LANES
        assert obs_here % (self.win * LANES) == 0


def pack_kernel(z, steps, ens_hbm, wts_hbm, dif_hbm, cell_hbm, window_hbm, value_hbm, weight_hbm, out, *scratch):
    ens, wts, dif, cell, window, value, weight, obs, sems = scratch
    k = lax.axis_index("win")
    mine = pl.ds(k * z.vars_here, z.vars_here)
    copies = [
        pltpu.make_async_copy(source, target, sems.at[n])
        for n, (source, target) in enumerate([
            (dif_hbm.at[mine], dif),
            (ens_hbm.at[:, mine], ens),
            (cell_hbm, cell),
            (window_hbm, window),
            (value_hbm, value),
            (weight_hbm, weight),
            (wts_hbm, wts),
        ])
    ]
    for copy in copies:
        copy.start()
    copies[0].wait()
    per_block = LANES // z.own
    for reg in range(z.dif_regs):
        mine = range(reg * GROUPS, min(z.vars_here, (reg + 1) * GROUPS))
        at = z.dif_at + reg * ROWS
        for d, part in windows([dif[v] for v in mine], z.own):
            for block in range(z.mem):
                out[block * per_block + d, at : at + ROWS, :] = part
    copies[1].wait()
    units = [ens[m, v] for m in range(z.members_here) for v in range(z.vars_here)]
    for reg in range(z.ens_regs):
        for d, part in windows(units[reg * GROUPS : (reg + 1) * GROUPS], z.own):
            out[d, reg * ROWS : (reg + 1) * ROWS, :] = part
    for copy in copies[2:]:
        copy.wait()
    count = jnp.full((ROWS, LANES), steps[0], jnp.int32).astype(jnp.float32)
    holds_weights = lane_ids() // SPAN < z.members_here
    for d, part in windows([wts[0, m] for m in range(z.members_here)], z.own):
        out[d, z.wts_at : z.wts_at + ROWS, :] = jnp.where(holds_weights, part, count)
    n = z.obs_rows
    for a, ref in enumerate((cell, window, value, weight)):
        rows = ref[0:n, :]
        for other in range(1, z.win):
            rows = jnp.where(k == other, ref[other * n : (other + 1) * n, :], rows)
        obs[a * n : (a + 1) * n, :] = rows.astype(jnp.float32)
    table = obs[...]
    for d in range(z.devices):
        out[d, z.obs_at :, :] = table


def spread4(first, second):
    group = lane_ids() // SPAN
    low, even = group < 2, group % 2 == 0
    a = jnp.where(even, first, roll(second, SPAN, 1))
    b = jnp.where(even, roll(first, -SPAN, 1), second)
    a2, b2 = roll(a, 64, 1), roll(b, 64, 1)
    return [jnp.where(low, a, a2), jnp.where(low, b, b2), jnp.where(low, a2, a), jnp.where(low, b2, b)]


def place(pieces, width):
    target = lane_ids() // width
    out = None
    for g, (x, lane) in enumerate(pieces):
        moved = roll(x, width * g - lane, 1)
        out = moved if out is None else jnp.where(target == g, moved, out)
    return out


def split3(x):
    high = x.astype(jnp.bfloat16).astype(jnp.float32)
    middle = (x - high).astype(jnp.bfloat16).astype(jnp.float32)
    return high, middle, x - high - middle


def descend_kernel(z, scale, coup, error_weight, recv, out, ens, dif, slope, bias):
    i, j, k = (lax.axis_index(a) for a in ("mem", "lat", "win"))
    d = (i * z.lat + j) * z.win + k
    start = lax.rem(d * z.own - z.halo + z.lon, z.lon)
    left = lax.div(start, LANES)
    right = lax.div(lax.rem(start + SPAN - 1, z.lon), LANES)
    lanes = lane_ids()
    sub = lax.broadcasted_iota(jnp.int32, (ROWS, LANES), 0)
    group = lanes // SPAN
    upper = group % 2 == 0
    in_left = start + lanes % SPAN < (left + 1) * LANES
    T, NV, M = z.tiles, z.variables, z.members

    def source(mem, lat, win):
        return (mem * z.lat + lat) * z.win + win

    for mem in range(z.mem):
        for win in range(z.win):
            for reg in range(z.ens_regs):
                for t in range(T):
                    got = spread4(*(recv[source(mem, h * T + t, win), reg * ROWS : (reg + 1) * ROWS, :] for h in range(2)))
                    for u, part in enumerate(got):
                        unit = reg * GROUPS + u
                        if unit < z.members_here * z.vars_here:
                            m = mem * z.members_here + unit // z.vars_here
                            v = win * z.vars_here + unit % z.vars_here
                            ens[m, v, t] = part
    for win in range(z.win):
        for reg in range(z.dif_regs):
            rows = pl.ds(z.dif_at + reg * ROWS, ROWS)
            for t in range(T):
                both = [
                    jnp.where(in_left, recv[source(left, h * T + t, win), rows, :], recv[source(right, h * T + t, win), rows, :])
                    for h in range(2)
                ]
                for u, part in enumerate(spread4(*both)):
                    if reg * GROUPS + u < z.vars_here:
                        dif[win * z.vars_here + reg * GROUPS + u, t] = part

    def weights_of(mem, lat, win):
        return recv[source(mem, lat, win), z.wts_at : z.wts_at + ROWS, :]

    control = []
    for m in range(M):
        mem, unit = divmod(m, z.members_here)
        control.append([
            [
                place([(weights_of(mem, h * T + t, 2 * p + w), SPAN * unit) for w in range(2) for h in range(2)], SPAN)
                for t in range(T)
            ]
            for p in range(z.pairs)
        ])
    counts = [
        place([(weights_of(0, 0, 2 * p + w), SPAN * z.members_here) for w in range(2) for h in range(2)], SPAN).astype(jnp.int32)
        for p in range(z.pairs)
    ]

    row_id = lax.broadcasted_iota(jnp.int32, (NV * ROWS, LANES), 0)
    key_id = lax.broadcasted_iota(jnp.int32, (z.win * SPAN, LANES), 0)
    n = z.obs_rows
    for lat in range(z.lat):
        rows_hot, parts = [], [[] for _ in range(3)]
        for side, block in enumerate((left, right)):
            for win in range(z.win):
                table = recv[source(block, lat, win), z.obs_at :, :]
                where = table[0:n, :].astype(jnp.int32)
                weight = table[3 * n : 4 * n, :]
                weighted = weight * table[2 * n : 3 * n, :]
                lane = block * LANES + where % LANES - start
                lane = jnp.where(lane < 0, lane + z.lon, lane)
                inside = lane < SPAN
                if side == 1:
                    inside &= left != right
                key = jnp.where(inside, table[n : 2 * n, :].astype(jnp.int32) * SPAN + lane, -1)
                row = where // LANES
                splits = list(zip(split3(weight), split3(weighted)))
                for x in range(n):
                    one = slice(x, x + 1)
                    hit = jnp.broadcast_to(key[one], key_id.shape) == key_id
                    rows_hot.append(jnp.where(jnp.broadcast_to(row[one], row_id.shape) == row_id, 1.0, 0.0).astype(jnp.bfloat16))
                    for part, pair in zip(parts, splits):
                        part.append(
                            jnp.concatenate(
                                [jnp.where(hit, jnp.broadcast_to(y[one], hit.shape), 0.0).astype(jnp.bfloat16) for y in pair], 0
                            )
                        )
        hot = jnp.concatenate(rows_hot, 1)
        total = 0.0
        for part in reversed(parts):
            total += lax.dot_general(
                hot, jnp.concatenate(part, 1), (((1,), (1,)), ((), ())), preferred_element_type=jnp.float32
            )
        h, t = divmod(lat, T)
        for q, field in enumerate((slope, bias)):
            for p in range(z.pairs):
                for w in range(2):
                    lane = (q * z.win + 2 * p + w) * SPAN
                    tile, at = divmod(lane, LANES)
                    mine = group == 2 * w + h
                    for v in range(NV):
                        x = total[v * ROWS : (v + 1) * ROWS, tile * LANES : (tile + 1) * LANES]
                        x = roll(x, SPAN * (2 * w + h) - at, 1)
                        if w == 0 and h == 0:
                            field[p, v, t] = x
                        else:
                            field[p, v, t] = jnp.where(mine, x, field[p, v, t])

    first, last = sub == 0, sub == ROWS - 1

    def beside(x):
        down = [roll(a, 1, 0) for a in x]
        up = [roll(a, -1, 0) for a in x]
        before_first = jnp.where(upper, 0.0, roll(down[T - 1], SPAN, 1))
        after_last = jnp.where(upper, roll(up[0], -SPAN, 1), 0.0)
        return [
            jnp.where(first, down[t - 1] if t else before_first, down[t])
            + jnp.where(last, up[t + 1] if t < T - 1 else after_last, up[t])
            for t in range(T)
        ]

    def smooth(x):
        for _ in range(DIFF):
            x = [
                a + KAPPA * (rows + roll(a, 1, 1) + roll(a, -1, 1) - 4.0 * a)
                for a, rows in zip(x, beside(x))
            ]
        return x

    def weigh(terms):
        total = None
        for factor, x in terms:
            total = factor * x if total is None else total + factor * x
        return total

    def forward(state, p, most):
        def step(section, flat):
            u = [list(flat[v * T : (v + 1) * T]) for v in range(NV)]
            on = section < counts[p]
            moved = []
            for v in range(NV):
                near = beside(u[v])
                for t in range(T):
                    x = u[v][t]
                    y = x + dif[v, t] * (near[t] - 2.0 * x) + weigh((coup[v, w], u[w][t]) for w in range(NV))
                    moved.append(jnp.where(on, y, x))
            return tuple(moved)

        flat = lax.fori_loop(0, most, step, tuple(x for v in state for x in v))
        return [list(flat[v * T : (v + 1) * T]) for v in range(NV)]

    def backward(state, p, most):
        def step(section, flat):
            u = [list(flat[v * T : (v + 1) * T]) for v in range(NV)]
            on = section < counts[p]
            moved = []
            for v in range(NV):
                weighted = [dif[v, t] * u[v][t] for t in range(T)]
                near = beside(weighted)
                for t in range(T):
                    x = u[v][t]
                    y = x + (near[t] - 2.0 * weighted[t]) + weigh((coup[w, v], u[w][t]) for w in range(NV))
                    moved.append(jnp.where(on, y, x))
            return tuple(moved)

        flat = lax.fori_loop(0, most, step, tuple(x for v in state for x in v))
        return [list(flat[v * T : (v + 1) * T]) for v in range(NV)]

    most = [jnp.max(c) for c in counts]
    later = group >= 2
    zero = jnp.zeros((ROWS, LANES), jnp.float32)
    for _ in range(ITERS):
        increment, ends = [], []
        smoothed = [[smooth(control[m][p]) for p in range(z.pairs)] for m in range(M)]
        for p in range(z.pairs):
            increment.append(
                [[weigh((ens[m, v, t], smoothed[m][p][t]) for m in range(M)) * scale for t in range(T)] for v in range(NV)]
            )
            ends.append(forward(increment[p], p, most[p]))
        misfit = []
        for p in range(z.pairs):
            misfit.append([])
            for v in range(NV):
                misfit[p].append([])
                for t in range(T):
                    before = roll(ends[p][v][t], 64, 1)
                    if p:
                        before = jnp.where(later, before, roll(ends[p - 1][v][t], 64, 1))
                    x = error_weight[v] * (before - increment[p][v][t])
                    misfit[p][v].append(x if p else jnp.where(later, x, 0.0))
        members_back = [[] for _ in range(M)]
        for p in range(z.pairs):
            forcing = []
            for v in range(NV):
                forcing.append([])
                for t in range(T):
                    after = roll(misfit[p + 1][v][t], 64, 1) if p + 1 < z.pairs else zero
                    after = jnp.where(later, after, roll(misfit[p][v][t], 64, 1))
                    forcing[v].append(slope[p, v, t] * ends[p][v][t] - bias[p, v, t] + after)
            adjoint = backward(forcing, p, most[p])
            gradient = [[adjoint[v][t] - misfit[p][v][t] for t in range(T)] for v in range(NV)]
            for m in range(M):
                members_back[m].append(
                    [weigh((ens[m, v, t], gradient[v][t]) for v in range(NV)) * scale for t in range(T)]
                )
        for m in range(M):
            for p in range(z.pairs):
                pulled = smooth(members_back[m][p])
                control[m][p] = [c - DESCENT * (c + x) for c, x in zip(control[m][p], pulled)]

    for lat in range(z.lat):
        h, t = divmod(lat, T)
        for win in range(z.win):
            p, w = divmod(win, 2)
            lane = SPAN * (2 * w + h) + z.halo
            grown = place([(increment[p][v][t], lane) for v in range(NV)], z.own)
            for mem in range(z.mem):
                to = source(mem, lat, win)
                mine = [control[mem * z.members_here + m][p][t] for m in range(z.members_here)]
                out[to, 0:ROWS, :] = place([(x, lane) for x in mine], z.own)
                out[to, ROWS : 2 * ROWS, :] = grown


def unpack_kernel(z, recv, control, increment):
    per_tile = LANES // z.own
    for m in range(z.members_here):
        for tile in range(z.lon // LANES):
            control[0, m, :, tile * LANES : (tile + 1) * LANES] = place(
                [(recv[tile * per_tile + q, 0:ROWS, :], z.own * m) for q in range(per_tile)], z.own
            )
    i = lax.axis_index("mem")
    for v in range(z.variables):
        increment[0, v] = place(
            [(recv[i * per_tile + q, ROWS : 2 * ROWS, :], z.own * v) for q in range(per_tile)], z.own
        )


def solution(mesh):
    smem = pl.BlockSpec(memory_space=pltpu.SMEM)
    vmem = pl.BlockSpec(memory_space=pltpu.VMEM)
    hbm = pl.BlockSpec(memory_space=pltpu.HBM)
    limit = 24 << 20
    f32 = jnp.float32

    def local(ensemble, weights, diffusivity, coupling, tl_steps, obs_cell, obs_window, obs_value, obs_weight, error_weight):
        z = Sizes(mesh.shape, ensemble.shape[0], ensemble.shape[1], ensemble.shape[3], obs_cell.shape[0])
        scale = 1.0 / math.sqrt(z.members - 1)
        axes = ("mem", "lat", "win")
        tables = [x.reshape(-1, LANES) for x in (obs_cell, obs_window, obs_value, obs_weight)]
        sent = pl.pallas_call(
            lambda *refs: pack_kernel(z, *refs),
            out_shape=jax.ShapeDtypeStruct((z.devices, z.chunk, LANES), f32),
            in_specs=[smem] + [hbm] * 7,
            out_specs=vmem,
            scratch_shapes=[
                pltpu.VMEM((z.members_here, z.vars_here, ROWS, z.lon), f32),
                pltpu.VMEM(weights.shape, f32),
                pltpu.VMEM((z.vars_here, ROWS, LANES), f32),
                *(pltpu.VMEM(x.shape, x.dtype) for x in tables),
                pltpu.VMEM((ROWS * z.obs_regs, LANES), f32),
                pltpu.SemaphoreType.DMA((7,)),
            ],
            compiler_params=pltpu.CompilerParams(vmem_limit_bytes=limit),
            name="pack",
        )(tl_steps, *(pltpu.with_memory_space_constraint(x, pltpu.HBM) for x in (ensemble, weights, diffusivity, *tables)))
        got = lax.all_to_all(sent, axes, 0, 0)
        field = pltpu.VMEM((z.pairs, z.variables, z.tiles, ROWS, LANES), f32)
        back = pl.pallas_call(
            lambda *refs: descend_kernel(z, scale, *refs),
            out_shape=jax.ShapeDtypeStruct((z.devices, 2 * ROWS, LANES), f32),
            in_specs=[smem, smem, vmem],
            out_specs=vmem,
            scratch_shapes=[
                pltpu.VMEM((z.members, z.variables, z.tiles, ROWS, LANES), f32),
                pltpu.VMEM((z.variables, z.tiles, ROWS, LANES), f32),
                field,
                field,
            ],
            compiler_params=pltpu.CompilerParams(vmem_limit_bytes=limit),
            name="descend",
        )(coupling, error_weight, got)
        home = lax.all_to_all(back, axes, 0, 0)
        return pl.pallas_call(
            lambda *refs: unpack_kernel(z, *refs),
            out_shape=(
                jax.ShapeDtypeStruct(weights.shape, f32),
                jax.ShapeDtypeStruct((1, z.variables, ROWS, LANES), f32),
            ),
            in_specs=[vmem],
            out_specs=(vmem, vmem),
            compiler_params=pltpu.CompilerParams(vmem_limit_bytes=limit),
            name="unpack",
        )(home)

    return jax.shard_map(
        local,
        mesh=mesh,
        in_specs=(
            P("mem", None, "lat", None),
            P("win", "mem", "lat", None),
            P(None, "lat", "mem"),
            P(),
            P("win"),
            P(("mem", "lat")),
            P(("mem", "lat")),
            P(("mem", "lat")),
            P(("mem", "lat")),
            P(),
        ),
        out_specs=(P("win", "mem", "lat", None), P("win", None, "lat", "mem")),
        check_vma=False,
    )
```

```python
import math

import jax
import jax.numpy as jnp
from jax import lax
from jax.experimental import pallas as pl
from jax.experimental.pallas import tpu as pltpu
from jax.sharding import PartitionSpec as P

KMAX = 6
DIFF = 2
ITERS = 2
KAPPA = 0.125
DESCENT = 0.25

ROWS = 8
LANES = 128
SPAN = 32
GROUPS = LANES // SPAN
HALF = ROWS // 2
PAIR = ROWS // GROUPS


def roll(x, shift, axis):
    shift %= x.shape[axis]
    return x if shift == 0 else pltpu.roll(x, shift, axis)


def lane_ids():
    return lax.broadcasted_iota(jnp.int32, (ROWS, LANES), 1)


def pad4(units):
    return list(units) + [jnp.zeros_like(units[0])] * (GROUPS - len(units))


def exchange4(x):
    group = lane_ids() // SPAN
    low, even = group < 2, group % 2 == 0
    a = [jnp.where(low, x[u], roll(x[u + 2], 64, 1)) for u in range(2)]
    b = [jnp.where(low, roll(x[u], 64, 1), x[u + 2]) for u in range(2)]
    out = []
    for first, second in (a, b):
        out.append(jnp.where(even, first, roll(second, SPAN, 1)))
        out.append(jnp.where(even, roll(first, -SPAN, 1), second))
    return out


def windows(units, own):
    halo, phases, length = (SPAN - own) // 2, SPAN // own, units[0].shape[1]
    for phase in range(phases):
        moved = pad4([roll(u, halo - own * phase, 1) for u in units])
        for tile in range(length // LANES):
            parts = exchange4([m[:, tile * LANES : (tile + 1) * LANES] for m in moved])
            for q, part in enumerate(parts):
                yield (tile * GROUPS + q) * phases + phase, part


class Sizes:
    def __init__(self, mesh_shape, members_here, variables, lon, obs_here):
        self.mem, self.lat, self.win = (mesh_shape[a] for a in ("mem", "lat", "win"))
        self.devices = self.mem * self.lat * self.win
        self.members_here, self.variables, self.lon = members_here, variables, lon
        self.members = members_here * self.mem
        self.vars_here = variables // self.win
        self.own = lon // self.devices
        self.halo = (SPAN - self.own) // 2
        self.tiles = self.lat // 2
        self.pairs = self.win // 2
        self.obs_rows = obs_here // self.win // LANES
        self.ens_regs = pl.cdiv(members_here * self.vars_here, GROUPS)
        self.dif_regs = pl.cdiv(self.vars_here, GROUPS)
        self.dif_at = ROWS * self.ens_regs
        self.wts_at = self.dif_at + ROWS * self.dif_regs
        self.obs_at = self.wts_at + HALF
        self.chunk = self.obs_at + 4 * self.obs_rows
        self.back = PAIR + ROWS
        assert lon // self.mem == LANES and members_here * SPAN <= LANES // 2 and members_here * self.own <= SPAN
        assert self.chunk % HALF == 0
        assert self.halo >= 2 * DIFF * ITERS
        assert self.lat % 2 == 0 and self.win % 2 == 0 and variables % self.win == 0
        assert SPAN % self.own == 0 and variables * self.own <= LANES
        assert obs_here % (self.win * LANES) == 0


def pack_kernel(z, steps, *refs):
    sources, (out, coup, error), scratch, sems = refs[:9], refs[9:12], refs[12:21], refs[21]
    coupling_in, error_in, dif, ens, cell, window, value, weight, wts = scratch
    k = lax.axis_index("win")
    mine = pl.ds(k * z.vars_here, z.vars_here)
    copies = []
    for n, (source, target) in enumerate(zip(sources, scratch)):
        source = source.at[mine] if target is dif else source.at[:, mine] if target is ens else source
        copies.append(pltpu.make_async_copy(source, target, sems.at[n]))
        copies[-1].start()
    copies[0].wait()
    copies[1].wait()
    for v in range(z.variables):
        error[v] = jnp.broadcast_to(error_in[:, v : v + 1], (ROWS, LANES))
        for w in range(z.variables):
            coup[v, w] = jnp.broadcast_to(coupling_in[v : v + 1, w : w + 1], (ROWS, LANES))
    copies[2].wait()
    per_block = LANES // z.own
    count = jnp.full((ROWS, LANES), steps[0], jnp.int32).astype(jnp.float32)
    spare = lane_ids() % SPAN == 0
    for reg in range(z.dif_regs):
        mine = range(reg * GROUPS, min(z.vars_here, (reg + 1) * GROUPS))
        for d, part in windows([dif[v] for v in mine], z.own):
            part = jnp.where(spare, count, part)
            for block in range(z.mem):
                at = (block * per_block + d) * z.chunk + z.dif_at + reg * ROWS
                out[at : at + ROWS, :] = part
    copies[3].wait()
    units = [ens[m, v] for m in range(z.members_here) for v in range(z.vars_here)]
    for reg in range(z.ens_regs):
        for d, part in windows(units[reg * GROUPS : (reg + 1) * GROUPS], z.own):
            at = d * z.chunk + reg * ROWS
            out[at : at + ROWS, :] = part
    for copy in copies[4:]:
        copy.wait()
    low = lane_ids() < LANES // 2
    for d, part in windows([wts[0, m] for m in range(z.members_here)], z.own):
        at = d * z.chunk + z.wts_at
        out[at : at + HALF, :] = jnp.where(low, part, roll(roll(part, LANES // 2, 1), HALF, 0))[:HALF]
    n = z.obs_rows
    for a, ref in enumerate((cell, window, value, weight)):
        rows = ref[0:n, :]
        for other in range(1, z.win):
            rows = jnp.where(k == other, ref[other * n : (other + 1) * n, :], rows)
        rows = rows.astype(jnp.float32)
        for d in range(z.devices):
            at = d * z.chunk + z.obs_at + a * n
            out[at : at + n, :] = rows


def spread4(first, second):
    group = lane_ids() // SPAN
    low, even = group < 2, group % 2 == 0
    a = jnp.where(even, first, roll(second, SPAN, 1))
    b = jnp.where(even, roll(first, -SPAN, 1), second)
    a2, b2 = roll(a, 64, 1), roll(b, 64, 1)
    return [jnp.where(low, a, a2), jnp.where(low, b, b2), jnp.where(low, a2, a), jnp.where(low, b2, b)]


def place(pieces, width):
    target = lax.broadcasted_iota(jnp.int32, pieces[0][0].shape, 1) // width
    out = None
    for g, (x, lane) in enumerate(pieces):
        moved = roll(x, width * g - lane, 1)
        out = moved if out is None else jnp.where(target == g, moved, out)
    return out


def split(x):
    high = x.astype(jnp.bfloat16).astype(jnp.float32)
    return high, x - high


def descend_kernel(z, scale, coup, error_weight, recv, out, ens, dif, own, slope, bias):
    i, j, k = (lax.axis_index(a) for a in ("mem", "lat", "win"))
    d = (i * z.lat + j) * z.win + k
    start = lax.rem(d * z.own - z.halo + z.lon, z.lon)
    left = lax.div(start, LANES)
    right = lax.div(lax.rem(start + SPAN - 1, z.lon), LANES)
    lanes = lane_ids()
    sub = lax.broadcasted_iota(jnp.int32, (ROWS, LANES), 0)
    group = lanes // SPAN
    upper = group % 2 == 0
    in_left = start + lanes % SPAN < (left + 1) * LANES
    T, NV, M = z.tiles, z.variables, z.members

    def source(mem, lat, win):
        return (mem * z.lat + lat) * z.win + win

    def take(mem, lat, win, at, rows):
        first = source(mem, lat, win) * z.chunk
        return recv[pl.ds((first if isinstance(first, int) else pl.multiple_of(first, HALF)) + at, rows), :]

    for mem in range(z.mem):
        for win in range(z.win):
            for reg in range(z.ens_regs):
                for t in range(T):
                    got = spread4(*(take(mem, h * T + t, win, reg * ROWS, ROWS) for h in range(2)))
                    for u, part in enumerate(got):
                        unit = reg * GROUPS + u
                        if unit < z.members_here * z.vars_here:
                            m = mem * z.members_here + unit // z.vars_here
                            v = win * z.vars_here + unit % z.vars_here
                            ens[m, v, t] = part
    for win in range(z.win):
        for reg in range(z.dif_regs):
            at = z.dif_at + reg * ROWS
            for t in range(T):
                both = [
                    jnp.where(in_left, take(left, h * T + t, win, at, ROWS), take(right, h * T + t, win, at, ROWS))
                    for h in range(2)
                ]
                for u, part in enumerate(spread4(*both)):
                    if reg * GROUPS + u < z.vars_here:
                        dif[win * z.vars_here + reg * GROUPS + u, t] = jnp.where(lanes % SPAN == 0, 0.0, part)

    def weights_of(mem, lat, win):
        x = take(mem, lat, win, z.wts_at, HALF)
        return jnp.concatenate([x, roll(x, LANES // 2, 1)], 0)

    control = [[[None] * T for _ in range(z.pairs)] for _ in range(M)]
    for mem in range(z.mem):
        for p in range(z.pairs):
            for t in range(T):
                quarter = [weights_of(mem, h * T + t, 2 * p + w) for w in range(2) for h in range(2)]
                for unit in range(z.members_here):
                    control[mem * z.members_here + unit][p][t] = place([(x, SPAN * unit) for x in quarter], SPAN)
    steps = [jnp.broadcast_to(take(0, 0, win, z.dif_at, 1)[:, :1], (ROWS, LANES)) for win in range(z.win)]
    counts = [jnp.where(group < 2, steps[2 * p], steps[2 * p + 1]).astype(jnp.int32) for p in range(z.pairs)]

    bf16 = jnp.bfloat16
    row_id = lax.broadcasted_iota(jnp.int32, (z.win * NV * ROWS, LANES), 0).astype(jnp.float32).astype(bf16)
    lane_id = lax.broadcasted_iota(jnp.int32, (SPAN, LANES), 0).astype(jnp.float32).astype(bf16)
    one, none = jnp.ones((), bf16), jnp.zeros((), bf16)
    n = z.obs_rows

    def column(x, like):
        return jnp.broadcast_to(x, like.shape).astype(bf16)

    for lat in range(z.lat):
        hot, parts = [], []
        for side, block in enumerate((left, right)):
            for win in range(z.win):
                where, time, value, weight = (take(block, lat, win, z.obs_at + a * n, n) for a in range(4))
                where = where.astype(jnp.int32)
                weighted = weight * value
                lane = block * LANES + where % LANES - start
                lane = jnp.where(lane < 0, lane + z.lon, lane)
                inside = lane < SPAN
                if side == 1:
                    inside &= left != right
                lane = jnp.where(inside, lane, -1).astype(jnp.float32)
                row = time * (NV * ROWS) + (where // LANES).astype(jnp.float32)
                values = [x for pair in zip(split(weight), split(weighted)) for x in pair]
                for x in range(n):
                    at = slice(x, x + 1)
                    hit = column(lane[at], lane_id) == lane_id
                    hot.append(jnp.where(column(row[at], row_id) == row_id, one, none))
                    parts.append(jnp.concatenate([jnp.where(hit, column(y[at], lane_id), none) for y in values], 0))
        total = lax.dot_general(
            jnp.concatenate(hot, 1),
            jnp.concatenate(parts, 1),
            (((1,), (1,)), ((), ())),
            preferred_element_type=jnp.float32,
        )
        h, t = divmod(lat, T)
        for p in range(z.pairs):
            for v in range(NV):
                sums = []
                for w in range(2):
                    at = ((2 * p + w) * NV + v) * ROWS
                    x = total[at : at + ROWS, :]
                    sums.append(x + roll(x, 2 * SPAN, 1))
                both = jnp.where(group < 2, sums[0], sums[1])
                x, y = (both, roll(both, -SPAN, 1)) if h == 0 else (roll(both, SPAN, 1), both)
                if h == 0:
                    slope[p, v, t], bias[p, v, t] = x, y
                else:
                    slope[p, v, t] = jnp.where(upper, slope[p, v, t], x)
                    bias[p, v, t] = jnp.where(upper, bias[p, v, t], y)

    first, last = sub == 0, sub == ROWS - 1

    def beside(x):
        down = [roll(a, 1, 0) for a in x]
        up = [roll(a, -1, 0) for a in x]
        before_first = jnp.where(upper, 0.0, roll(down[T - 1], SPAN, 1))
        after_last = jnp.where(upper, roll(up[0], -SPAN, 1), 0.0)
        return [
            jnp.where(first, down[t - 1] if t else before_first, down[t])
            + jnp.where(last, up[t + 1] if t < T - 1 else after_last, up[t])
            for t in range(T)
        ]

    def smooth(x):
        for _ in range(DIFF):
            x = [
                (1.0 - 4.0 * KAPPA) * a + KAPPA * (rows + roll(a, 1, 1) + roll(a, -1, 1))
                for a, rows in zip(x, beside(x))
            ]
        return x

    def weigh(terms):
        total = None
        for factor, x in terms:
            total = factor * x if total is None else total + factor * x
        return total

    for v in range(NV):
        for t in range(T):
            own[v, t] = 1.0 - 2.0 * dif[v, t] + coup[v, v]

    def repeat(step, state, p):
        def section(index, flat):
            moved = step([list(flat[v * T : (v + 1) * T]) for v in range(NV)])
            on = index < counts[p]
            return tuple(jnp.where(on, x, y) for x, y in zip((x for v in moved for x in v), flat))

        flat = lax.fori_loop(0, most[p], section, tuple(x for v in state for x in v))
        return [list(flat[v * T : (v + 1) * T]) for v in range(NV)]

    def forward(u):
        moved = []
        for v in range(NV):
            near = beside(u[v])
            moved.append([
                own[v, t] * u[v][t] + dif[v, t] * near[t] + weigh((coup[v, w], u[w][t]) for w in range(NV) if w != v)
                for t in range(T)
            ])
        return moved

    def backward(u):
        moved = []
        for v in range(NV):
            near = beside([dif[v, t] * u[v][t] for t in range(T)])
            moved.append([
                own[v, t] * u[v][t] + near[t] + weigh((coup[w, v], u[w][t]) for w in range(NV) if w != v) for t in range(T)
            ])
        return moved

    most = [jnp.max(c) for c in counts]
    later = group >= 2
    zero = jnp.zeros((ROWS, LANES), jnp.float32)
    for _ in range(ITERS):
        increment, ends = [], []
        smoothed = [[smooth(control[m][p]) for p in range(z.pairs)] for m in range(M)]
        for p in range(z.pairs):
            increment.append(
                [[weigh((ens[m, v, t], smoothed[m][p][t]) for m in range(M)) * scale for t in range(T)] for v in range(NV)]
            )
            ends.append(repeat(forward, increment[p], p))
        misfit = []
        for p in range(z.pairs):
            misfit.append([])
            for v in range(NV):
                misfit[p].append([])
                for t in range(T):
                    before = roll(ends[p][v][t], 64, 1)
                    if p:
                        before = jnp.where(later, before, roll(ends[p - 1][v][t], 64, 1))
                    x = error_weight[v] * (before - increment[p][v][t])
                    misfit[p][v].append(x if p else jnp.where(later, x, 0.0))
        members_back = [[] for _ in range(M)]
        for p in range(z.pairs):
            forcing = []
            for v in range(NV):
                forcing.append([])
                for t in range(T):
                    after = roll(misfit[p + 1][v][t], 64, 1) if p + 1 < z.pairs else zero
                    after = jnp.where(later, after, roll(misfit[p][v][t], 64, 1))
                    forcing[v].append(slope[p, v, t] * ends[p][v][t] - bias[p, v, t] + after)
            adjoint = repeat(backward, forcing, p)
            gradient = [[adjoint[v][t] - misfit[p][v][t] for t in range(T)] for v in range(NV)]
            for m in range(M):
                members_back[m].append(
                    [weigh((ens[m, v, t], gradient[v][t]) for v in range(NV)) * scale for t in range(T)]
                )
        for m in range(M):
            for p in range(z.pairs):
                pulled = smooth(members_back[m][p])
                control[m][p] = [c - DESCENT * (c + x) for c, x in zip(control[m][p], pulled)]

    for lat in range(z.lat):
        h, t = divmod(lat, T)
        for win in range(z.win):
            p, w = divmod(win, 2)
            lane = SPAN * (2 * w + h) + z.halo
            grown = place([(increment[p][v][t], lane) for v in range(NV)], z.own)
            for mem in range(z.mem):
                to = source(mem, lat, win)
                mine = [control[mem * z.members_here + m][p][t] for m in range(z.members_here)]
                x = place([(x, lane) for x in mine], z.own)
                folded = place([(roll(x, -PAIR * q, 0), 0) for q in range(GROUPS)], SPAN)
                out[to * z.back : to * z.back + PAIR, :] = folded[:PAIR]
                out[to * z.back + PAIR : (to + 1) * z.back, :] = grown


def unpack_kernel(z, recv, control, increment):
    per_tile = LANES // z.own
    for tile in range(z.lon // LANES):
        got = [recv[d * z.back : d * z.back + PAIR, :] for d in range(tile * per_tile, (tile + 1) * per_tile)]
        for m in range(z.members_here):
            for q in range(GROUPS):
                control[0, m, PAIR * q : PAIR * (q + 1), tile * LANES : (tile + 1) * LANES] = place(
                    [(x, SPAN * q + z.own * m) for x in got], z.own
                )
    first = lax.axis_index("mem") * per_tile
    got = [recv[pl.ds(pl.multiple_of((first + q) * z.back, PAIR) + PAIR, ROWS), :] for q in range(per_tile)]
    for v in range(z.variables):
        increment[0, v] = place([(x, z.own * v) for x in got], z.own)


def in_hbm(*arrays):
    return [pltpu.with_memory_space_constraint(x, pltpu.HBM) for x in arrays]


def solution(mesh):
    smem = pl.BlockSpec(memory_space=pltpu.SMEM)
    vmem = pl.BlockSpec(memory_space=pltpu.VMEM)
    hbm = pl.BlockSpec(memory_space=pltpu.HBM)
    f32 = jnp.float32

    def local(ensemble, weights, diffusivity, coupling, tl_steps, obs_cell, obs_window, obs_value, obs_weight, error_weight):
        z = Sizes(mesh.shape, ensemble.shape[0], ensemble.shape[1], ensemble.shape[3], obs_cell.shape[0])
        scale = 1.0 / math.sqrt(z.members - 1)
        tables = [x.reshape(-1, LANES) for x in (obs_cell, obs_window, obs_value, obs_weight)]
        params = pltpu.CompilerParams(vmem_limit_bytes=24 << 20)
        reg = (ROWS, LANES)
        field = pltpu.VMEM((z.pairs, z.variables, z.tiles, *reg), f32)
        still = pltpu.VMEM((z.variables, z.tiles, *reg), f32)

        def exchange(x, rows):
            step = math.gcd(rows, ROWS)
            split = x.reshape(z.devices, rows // step, step, LANES)
            return lax.all_to_all(split, ("mem", "lat", "win"), 0, 0).reshape(x.shape)

        sent, coup, error = pl.pallas_call(
            lambda *refs: pack_kernel(z, *refs),
            out_shape=(
                jax.ShapeDtypeStruct((z.devices * z.chunk, LANES), f32),
                jax.ShapeDtypeStruct((z.variables, z.variables, *reg), f32),
                jax.ShapeDtypeStruct((z.variables, *reg), f32),
            ),
            in_specs=[smem] + [hbm] * 9,
            out_specs=(vmem, vmem, vmem),
            scratch_shapes=[
                pltpu.VMEM(coupling.shape, f32),
                pltpu.VMEM((1, z.variables), f32),
                pltpu.VMEM((z.vars_here, *reg), f32),
                pltpu.VMEM((z.members_here, z.vars_here, ROWS, z.lon), f32),
                *(pltpu.VMEM(x.shape, x.dtype) for x in tables),
                pltpu.VMEM(weights.shape, f32),
                pltpu.SemaphoreType.DMA((9,)),
            ],
            compiler_params=params,
            name="pack",
        )(tl_steps, *in_hbm(coupling, error_weight.reshape(1, -1), diffusivity, ensemble, *tables, weights))
        back = pl.pallas_call(
            lambda *refs: descend_kernel(z, scale, *refs),
            out_shape=jax.ShapeDtypeStruct((z.devices * z.back, LANES), f32),
            in_specs=[vmem, vmem, vmem],
            out_specs=vmem,
            scratch_shapes=[
                pltpu.VMEM((z.members, z.variables, z.tiles, *reg), f32),
                still,
                still,
                field,
                field,
            ],
            compiler_params=params,
            name="descend",
        )(coup, error, exchange(sent, z.chunk))
        home = exchange(back, z.back)
        return pl.pallas_call(
            lambda *refs: unpack_kernel(z, *refs),
            out_shape=(
                jax.ShapeDtypeStruct(weights.shape, f32),
                jax.ShapeDtypeStruct((1, z.variables, ROWS, LANES), f32),
            ),
            in_specs=[vmem],
            out_specs=(vmem, vmem),
            compiler_params=params,
            name="unpack",
        )(home)

    return jax.shard_map(
        local,
        mesh=mesh,
        in_specs=(
            P("mem", None, "lat", None),
            P("win", "mem", "lat", None),
            P(None, "lat", "mem"),
            P(),
            P("win"),
            P(("mem", "lat")),
            P(("mem", "lat")),
            P(("mem", "lat")),
            P(("mem", "lat")),
            P(),
        ),
        out_specs=(P("win", "mem", "lat", None), P("win", None, "lat", "mem")),
        check_vma=False,
    )
```

```python
import math

import jax
import jax.numpy as jnp
from jax import lax
from jax.experimental import pallas as pl
from jax.experimental.pallas import tpu as pltpu
from jax.sharding import PartitionSpec as P

KMAX = 6
DIFF = 2
ITERS = 2
KAPPA = 0.125
DESCENT = 0.25

ROWS = 8
LANES = 128
SPAN = 32
GROUPS = LANES // SPAN
HALF = ROWS // 2
PAIR = ROWS // GROUPS


def roll(x, shift, axis):
    shift %= x.shape[axis]
    return x if shift == 0 else pltpu.roll(x, shift, axis)


def lane_ids():
    return lax.broadcasted_iota(jnp.int32, (ROWS, LANES), 1)


def pad4(units):
    return list(units) + [jnp.zeros_like(units[0])] * (GROUPS - len(units))


def exchange4(x):
    group = lane_ids() // SPAN
    low, even = group < 2, group % 2 == 0
    a = [jnp.where(low, x[u], roll(x[u + 2], 64, 1)) for u in range(2)]
    b = [jnp.where(low, roll(x[u], 64, 1), x[u + 2]) for u in range(2)]
    out = []
    for first, second in (a, b):
        out.append(jnp.where(even, first, roll(second, SPAN, 1)))
        out.append(jnp.where(even, roll(first, -SPAN, 1), second))
    return out


def windows(units, own):
    halo, phases, length = (SPAN - own) // 2, SPAN // own, units[0].shape[1]
    for phase in range(phases):
        moved = pad4([roll(u, halo - own * phase, 1) for u in units])
        for tile in range(length // LANES):
            parts = exchange4([m[:, tile * LANES : (tile + 1) * LANES] for m in moved])
            for q, part in enumerate(parts):
                yield (tile * GROUPS + q) * phases + phase, part


class Sizes:
    def __init__(self, mesh_shape, members_here, variables, lon, obs_here):
        self.mem, self.lat, self.win = (mesh_shape[a] for a in ("mem", "lat", "win"))
        self.devices = self.mem * self.lat * self.win
        self.members_here, self.variables, self.lon = members_here, variables, lon
        self.members = members_here * self.mem
        self.vars_here = variables // self.win
        self.own = lon // self.devices
        self.halo = (SPAN - self.own) // 2
        self.tiles = self.lat // 2
        self.pairs = self.win // 2
        self.obs_rows = obs_here // self.win // LANES
        self.ens_regs = pl.cdiv(members_here * self.vars_here, GROUPS)
        self.dif_regs = pl.cdiv(self.vars_here, GROUPS)
        self.dif_at = ROWS * self.ens_regs
        self.wts_at = self.dif_at + ROWS * self.dif_regs
        self.obs_at = self.wts_at + HALF
        self.chunk = self.obs_at + 4 * self.obs_rows
        self.back = PAIR + ROWS
        assert lon // self.mem == LANES and members_here * SPAN <= LANES // 2 and members_here * self.own <= SPAN
        assert self.chunk % HALF == 0
        assert self.halo >= 2 * DIFF * ITERS
        assert self.lat % 2 == 0 and self.win % 2 == 0 and variables % self.win == 0
        assert SPAN % self.own == 0 and variables * self.own <= LANES
        assert obs_here % (self.win * LANES) == 0

    def slot(self, d):
        mem, rest = divmod(d, self.lat * self.win)
        lat, win = divmod(rest, self.win)
        return (lat * self.mem + mem) * self.win + win


def turn(x):
    pair = lax.broadcasted_iota(jnp.int32, (ROWS, LANES), 0) // PAIR
    group = lane_ids() // SPAN
    x = jnp.where(pair // 2 == group // 2, x, roll(roll(x, LANES // 2, 1), HALF, 0))
    up, down = roll(roll(x, -PAIR, 0), SPAN, 1), roll(roll(x, PAIR, 0), -SPAN, 1)
    return jnp.where(pair % 2 == group % 2, x, jnp.where(pair % 2 == 0, up, down))


def pack_kernel(z, steps, *refs):
    sources, (out, coup, error), scratch, sems = refs[:9], refs[9:12], refs[12:21], refs[21]
    coupling_in, error_in, dif, ens, cell, window, value, weight, wts = scratch
    k = lax.axis_index("win")
    mine = pl.ds(k * z.vars_here, z.vars_here)
    copies = []
    for n, (source, target) in enumerate(zip(sources, scratch)):
        source = source.at[mine] if target is dif else source.at[:, mine] if target is ens else source
        copies.append(pltpu.make_async_copy(source, target, sems.at[n]))
        copies[-1].start()
    copies[0].wait()
    copies[1].wait()
    for v in range(z.variables):
        error[v] = jnp.broadcast_to(error_in[:, v : v + 1], (ROWS, LANES))
        for w in range(z.variables):
            coup[v, w] = jnp.broadcast_to(coupling_in[v : v + 1, w : w + 1], (ROWS, LANES))
    copies[2].wait()
    per_block = LANES // z.own
    count = jnp.full((ROWS, LANES), steps[0], jnp.int32).astype(jnp.float32)
    spare = lane_ids() % SPAN == 0
    for reg in range(z.dif_regs):
        mine = range(reg * GROUPS, min(z.vars_here, (reg + 1) * GROUPS))
        for d, part in windows([dif[v] for v in mine], z.own):
            part = jnp.where(spare, count, part)
            for block in range(z.mem):
                at = z.slot(block * per_block + d) * z.chunk + z.dif_at + reg * ROWS
                out[at : at + ROWS, :] = part
    for copy in copies[3:8]:
        copy.wait()
    n = z.obs_rows
    tables = []
    for ref in (cell, window, value, weight):
        rows = ref[0:n, :]
        for other in range(1, z.win):
            rows = jnp.where(k == other, ref[other * n : (other + 1) * n, :], rows)
        tables.append(rows.astype(jnp.float32))
    units = [ens[m, v] for m in range(z.members_here) for v in range(z.vars_here)]
    for reg in range(z.ens_regs):
        for d, part in windows(units[reg * GROUPS : (reg + 1) * GROUPS], z.own):
            at = z.slot(d) * z.chunk + reg * ROWS
            out[at : at + ROWS, :] = part
    copies[8].wait()
    low = lane_ids() < LANES // 2
    for d, part in windows([wts[0, m] for m in range(z.members_here)], z.own):
        at = z.slot(d) * z.chunk + z.wts_at
        out[at : at + HALF, :] = jnp.where(low, part, roll(roll(part, LANES // 2, 1), HALF, 0))[:HALF]
    for a, rows in enumerate(tables):
        for d in range(z.devices):
            at = d * z.chunk + z.obs_at + a * n
            out[at : at + n, :] = rows


def spread4(first, second):
    group = lane_ids() // SPAN
    low, even = group < 2, group % 2 == 0
    a = jnp.where(even, first, roll(second, SPAN, 1))
    b = jnp.where(even, roll(first, -SPAN, 1), second)
    a2, b2 = roll(a, 64, 1), roll(b, 64, 1)
    return [jnp.where(low, a, a2), jnp.where(low, b, b2), jnp.where(low, a2, a), jnp.where(low, b2, b)]


def place(pieces, width):
    block = lane_ids() // width
    out = None
    for x, source, target in pieces:
        moved = roll(x, target - source, 1)
        out = moved if out is None else jnp.where(block == target // width, moved, out)
    return out


def split(x):
    high = x.astype(jnp.bfloat16).astype(jnp.float32)
    return high, x - high


def descend_kernel(z, scale, coup, error_weight, recv, out, ens, dif, own, slope, bias):
    i, j, k = (lax.axis_index(a) for a in ("mem", "lat", "win"))
    d = (i * z.lat + j) * z.win + k
    start = lax.rem(d * z.own - z.halo + z.lon, z.lon)
    left = lax.div(start, LANES)
    right = lax.div(lax.rem(start + SPAN - 1, z.lon), LANES)
    lanes = lane_ids()
    sub = lax.broadcasted_iota(jnp.int32, (ROWS, LANES), 0)
    group = lanes // SPAN
    upper = group % 2 == 0
    in_left = start + lanes % SPAN < (left + 1) * LANES
    T, NV, M = z.tiles, z.variables, z.members

    def source(mem, lat, win):
        return (mem * z.lat + lat) * z.win + win

    def take(mem, lat, win, at, rows):
        first = ((lat * z.mem + mem) * z.win + win) * z.chunk
        return recv[pl.ds((first if isinstance(first, int) else pl.multiple_of(first, HALF)) + at, rows), :]

    for mem in range(z.mem):
        for win in range(z.win):
            for reg in range(z.ens_regs):
                for t in range(T):
                    got = spread4(*(take(mem, h * T + t, win, reg * ROWS, ROWS) for h in range(2)))
                    for u, part in enumerate(got):
                        unit = reg * GROUPS + u
                        if unit < z.members_here * z.vars_here:
                            m = mem * z.members_here + unit // z.vars_here
                            v = win * z.vars_here + unit % z.vars_here
                            ens[m, v, t] = part
    for win in range(z.win):
        for reg in range(z.dif_regs):
            at = z.dif_at + reg * ROWS
            for t in range(T):
                both = [
                    jnp.where(in_left, take(left, h * T + t, win, at, ROWS), take(right, h * T + t, win, at, ROWS))
                    for h in range(2)
                ]
                for u, part in enumerate(spread4(*both)):
                    if reg * GROUPS + u < z.vars_here:
                        dif[win * z.vars_here + reg * GROUPS + u, t] = jnp.where(lanes % SPAN == 0, 0.0, part)

    def weights_of(mem, lat, win):
        x = take(mem, lat, win, z.wts_at, HALF)
        return jnp.concatenate([x, roll(x, LANES // 2, 1)], 0)

    control = [[[None] * T for _ in range(z.pairs)] for _ in range(M)]
    for mem in range(z.mem):
        for p in range(z.pairs):
            for t in range(T):
                quarter = [weights_of(mem, h * T + t, 2 * p + w) for w in range(2) for h in range(2)]
                for unit in range(z.members_here):
                    control[mem * z.members_here + unit][p][t] = place([(x, SPAN * unit, SPAN * g) for g, x in enumerate(quarter)], SPAN)
    steps = [jnp.broadcast_to(take(0, 0, win, z.dif_at, 1)[:, :1], (ROWS, LANES)) for win in range(z.win)]
    counts = [jnp.where(group < 2, steps[2 * p], steps[2 * p + 1]).astype(jnp.int32) for p in range(z.pairs)]

    bf16 = jnp.bfloat16
    row_id = lax.broadcasted_iota(jnp.int32, (z.win * NV * ROWS, LANES), 0).astype(jnp.float32).astype(bf16)
    lane_id = lax.broadcasted_iota(jnp.int32, (SPAN, LANES), 0).astype(jnp.float32).astype(bf16)
    one, none = jnp.ones((), bf16), jnp.zeros((), bf16)
    n = z.obs_rows

    def column(x, like):
        return jnp.broadcast_to(x, like.shape).astype(bf16)

    for lat in range(z.lat):
        hot, parts = [], []
        for side, block in enumerate((left, right)):
            for win in range(z.win):
                where, time, value, weight = (take(block, lat, win, z.obs_at + a * n, n) for a in range(4))
                where = where.astype(jnp.int32)
                weighted = weight * value
                lane = block * LANES + where % LANES - start
                lane = jnp.where(lane < 0, lane + z.lon, lane)
                inside = lane < SPAN
                if side == 1:
                    inside &= left != right
                lane = jnp.where(inside, lane, -1).astype(jnp.float32)
                row = time * (NV * ROWS) + (where // LANES).astype(jnp.float32)
                values = [x for pair in zip(split(weight), split(weighted)) for x in pair]
                for x in range(n):
                    at = slice(x, x + 1)
                    hit = column(lane[at], lane_id) == lane_id
                    hot.append(jnp.where(column(row[at], row_id) == row_id, one, none))
                    parts.append(jnp.concatenate([jnp.where(hit, column(y[at], lane_id), none) for y in values], 0))
        total = lax.dot_general(
            jnp.concatenate(hot, 1),
            jnp.concatenate(parts, 1),
            (((1,), (1,)), ((), ())),
            preferred_element_type=jnp.float32,
        )
        h, t = divmod(lat, T)
        for p in range(z.pairs):
            for v in range(NV):
                sums = []
                for w in range(2):
                    at = ((2 * p + w) * NV + v) * ROWS
                    x = total[at : at + ROWS, :]
                    sums.append(x + roll(x, 2 * SPAN, 1))
                both = jnp.where(group < 2, sums[0], sums[1])
                x, y = (both, roll(both, -SPAN, 1)) if h == 0 else (roll(both, SPAN, 1), both)
                if h == 0:
                    slope[p, v, t], bias[p, v, t] = x, y
                else:
                    slope[p, v, t] = jnp.where(upper, slope[p, v, t], x)
                    bias[p, v, t] = jnp.where(upper, bias[p, v, t], y)

    first, last = sub == 0, sub == ROWS - 1

    def beside(x):
        down = [roll(a, 1, 0) for a in x]
        up = [roll(a, -1, 0) for a in x]
        before_first = jnp.where(upper, 0.0, roll(down[T - 1], SPAN, 1))
        after_last = jnp.where(upper, roll(up[0], -SPAN, 1), 0.0)
        return [
            jnp.where(first, down[t - 1] if t else before_first, down[t])
            + jnp.where(last, up[t + 1] if t < T - 1 else after_last, up[t])
            for t in range(T)
        ]

    def smooth(x):
        for _ in range(DIFF):
            x = [
                (1.0 - 4.0 * KAPPA) * a + KAPPA * (rows + roll(a, 1, 1) + roll(a, -1, 1))
                for a, rows in zip(x, beside(x))
            ]
        return x

    def weigh(terms):
        total = None
        for factor, x in terms:
            total = factor * x if total is None else total + factor * x
        return total

    for v in range(NV):
        for t in range(T):
            own[v, t] = 1.0 - 2.0 * dif[v, t] + coup[v, v]

    def repeat(step, state, p):
        def section(index, flat):
            moved = step([list(flat[v * T : (v + 1) * T]) for v in range(NV)])
            on = index < counts[p]
            return tuple(jnp.where(on, x, y) for x, y in zip((x for v in moved for x in v), flat))

        flat = lax.fori_loop(0, most[p], section, tuple(x for v in state for x in v))
        return [list(flat[v * T : (v + 1) * T]) for v in range(NV)]

    def forward(u):
        moved = []
        for v in range(NV):
            near = beside(u[v])
            moved.append([
                own[v, t] * u[v][t] + dif[v, t] * near[t] + weigh((coup[v, w], u[w][t]) for w in range(NV) if w != v)
                for t in range(T)
            ])
        return moved

    def backward(u):
        moved = []
        for v in range(NV):
            near = beside([dif[v, t] * u[v][t] for t in range(T)])
            moved.append([
                own[v, t] * u[v][t] + near[t] + weigh((coup[w, v], u[w][t]) for w in range(NV) if w != v) for t in range(T)
            ])
        return moved

    most = [jnp.max(c) for c in counts]
    later = group >= 2
    zero = jnp.zeros((ROWS, LANES), jnp.float32)
    for _ in range(ITERS):
        increment, ends = [], []
        smoothed = [[smooth(control[m][p]) for p in range(z.pairs)] for m in range(M)]
        for p in range(z.pairs):
            increment.append(
                [[weigh((ens[m, v, t], smoothed[m][p][t]) for m in range(M)) * scale for t in range(T)] for v in range(NV)]
            )
            ends.append(repeat(forward, increment[p], p))
        misfit = []
        for p in range(z.pairs):
            misfit.append([])
            for v in range(NV):
                misfit[p].append([])
                for t in range(T):
                    before = roll(ends[p][v][t], 64, 1)
                    if p:
                        before = jnp.where(later, before, roll(ends[p - 1][v][t], 64, 1))
                    x = error_weight[v] * (before - increment[p][v][t])
                    misfit[p][v].append(x if p else jnp.where(later, x, 0.0))
        members_back = [[] for _ in range(M)]
        for p in range(z.pairs):
            forcing = []
            for v in range(NV):
                forcing.append([])
                for t in range(T):
                    after = roll(misfit[p + 1][v][t], 64, 1) if p + 1 < z.pairs else zero
                    after = jnp.where(later, after, roll(misfit[p][v][t], 64, 1))
                    forcing[v].append(slope[p, v, t] * ends[p][v][t] - bias[p, v, t] + after)
            adjoint = repeat(backward, forcing, p)
            gradient = [[adjoint[v][t] - misfit[p][v][t] for t in range(T)] for v in range(NV)]
            for m in range(M):
                members_back[m].append(
                    [weigh((ens[m, v, t], gradient[v][t]) for v in range(NV)) * scale for t in range(T)]
                )
        for m in range(M):
            for p in range(z.pairs):
                pulled = smooth(members_back[m][p])
                control[m][p] = [c - DESCENT * (c + x) for c, x in zip(control[m][p], pulled)]

    for lat in range(z.lat):
        h, t = divmod(lat, T)
        for win in range(z.win):
            p, w = divmod(win, 2)
            lane = SPAN * (2 * w + h) + z.halo
            grown = place([(increment[p][v][t], lane, z.own * v) for v in range(NV)], z.own)
            for first_mem in range(0, z.mem, GROUPS):
                mems = range(first_mem, min(z.mem, first_mem + GROUPS))
                x = place(
                    [
                        (control[mem * z.members_here + m][p][t], lane, SPAN * (mem - first_mem) + z.own * m)
                        for mem in mems
                        for m in range(z.members_here)
                    ],
                    z.own,
                )
                x = turn(x)
                for mem in mems:
                    to, at = source(mem, lat, win) * z.back, PAIR * (mem - first_mem)
                    out[to : to + PAIR, :] = x[at : at + PAIR]
                    out[to + PAIR : to + z.back, :] = grown


def unpack_kernel(z, recv, control, increment):
    per_tile = LANES // z.own
    for tile in range(z.lon // LANES):
        pieces = []
        for batch in range(0, per_tile, GROUPS):
            x = turn(jnp.concatenate(
                [recv[d * z.back : d * z.back + PAIR, :] for d in range(tile * per_tile + batch, tile * per_tile + batch + GROUPS)], 0
            ))
            pieces += [(x, SPAN * g, z.own * (batch + g)) for g in range(GROUPS)]
        for m in range(z.members_here):
            control[0, m, :, tile * LANES : (tile + 1) * LANES] = place(
                [(x, source + z.own * m, target) for x, source, target in pieces], z.own
            )
    first = lax.axis_index("mem") * per_tile
    got = [recv[pl.ds(pl.multiple_of((first + q) * z.back, PAIR) + PAIR, ROWS), :] for q in range(per_tile)]
    for v in range(z.variables):
        increment[0, v] = place([(x, z.own * v, z.own * q) for q, x in enumerate(got)], z.own)


def in_hbm(*arrays):
    return [pltpu.with_memory_space_constraint(x, pltpu.HBM) for x in arrays]


def solution(mesh):
    smem = pl.BlockSpec(memory_space=pltpu.SMEM)
    vmem = pl.BlockSpec(memory_space=pltpu.VMEM)
    hbm = pl.BlockSpec(memory_space=pltpu.HBM)
    f32 = jnp.float32

    def local(ensemble, weights, diffusivity, coupling, tl_steps, obs_cell, obs_window, obs_value, obs_weight, error_weight):
        z = Sizes(mesh.shape, ensemble.shape[0], ensemble.shape[1], ensemble.shape[3], obs_cell.shape[0])
        scale = 1.0 / math.sqrt(z.members - 1)
        tables = [x.reshape(-1, LANES) for x in (obs_cell, obs_window, obs_value, obs_weight)]
        params = pltpu.CompilerParams(vmem_limit_bytes=24 << 20)
        reg = (ROWS, LANES)
        field = pltpu.VMEM((z.pairs, z.variables, z.tiles, *reg), f32)
        still = pltpu.VMEM((z.variables, z.tiles, *reg), f32)

        def exchange(x, rows, axes):
            step = math.gcd(rows, ROWS)
            split = x.reshape(z.devices, rows // step, step, LANES)
            return lax.all_to_all(split, axes, 0, 0).reshape(x.shape)

        sent, coup, error = pl.pallas_call(
            lambda *refs: pack_kernel(z, *refs),
            out_shape=(
                jax.ShapeDtypeStruct((z.devices * z.chunk, LANES), f32),
                jax.ShapeDtypeStruct((z.variables, z.variables, *reg), f32),
                jax.ShapeDtypeStruct((z.variables, *reg), f32),
            ),
            in_specs=[smem] + [hbm] * 9,
            out_specs=(vmem, vmem, vmem),
            scratch_shapes=[
                pltpu.VMEM(coupling.shape, f32),
                pltpu.VMEM((1, z.variables), f32),
                pltpu.VMEM((z.vars_here, *reg), f32),
                pltpu.VMEM((z.members_here, z.vars_here, ROWS, z.lon), f32),
                *(pltpu.VMEM(x.shape, x.dtype) for x in tables),
                pltpu.VMEM(weights.shape, f32),
                pltpu.SemaphoreType.DMA((9,)),
            ],
            compiler_params=params,
            name="pack",
        )(tl_steps, *in_hbm(coupling, error_weight.reshape(1, -1), diffusivity, ensemble, *tables, weights))
        back = pl.pallas_call(
            lambda *refs: descend_kernel(z, scale, *refs),
            out_shape=jax.ShapeDtypeStruct((z.devices * z.back, LANES), f32),
            in_specs=[vmem, vmem, vmem],
            out_specs=vmem,
            scratch_shapes=[
                pltpu.VMEM((z.members, z.variables, z.tiles, *reg), f32),
                still,
                still,
                field,
                field,
            ],
            compiler_params=params,
            name="descend",
        )(coup, error, exchange(sent, z.chunk, ("lat", "mem", "win")))
        home = exchange(back, z.back, ("mem", "lat", "win"))
        return pl.pallas_call(
            lambda *refs: unpack_kernel(z, *refs),
            out_shape=(
                jax.ShapeDtypeStruct(weights.shape, f32),
                jax.ShapeDtypeStruct((1, z.variables, ROWS, LANES), f32),
            ),
            in_specs=[vmem],
            out_specs=(vmem, vmem),
            compiler_params=params,
            name="unpack",
        )(home)

    return jax.shard_map(
        local,
        mesh=mesh,
        in_specs=(
            P("mem", None, "lat", None),
            P("win", "mem", "lat", None),
            P(None, "lat", "mem"),
            P(),
            P("win"),
            P(("mem", "lat")),
            P(("mem", "lat")),
            P(("mem", "lat")),
            P(("mem", "lat")),
            P(),
        ),
        out_specs=(P("win", "mem", "lat", None), P("win", None, "lat", "mem")),
        check_vma=False,
    )
```

```python
import math

import jax
import jax.numpy as jnp
from jax import lax
from jax.experimental import pallas as pl
from jax.experimental.pallas import tpu as pltpu
from jax.sharding import PartitionSpec as P

KMAX = 6
DIFF = 2
ITERS = 2
KAPPA = 0.125
DESCENT = 0.25

ROWS = 8
LANES = 128
SPAN = 32
GROUPS = LANES // SPAN
HALF = ROWS // 2
PAIR = ROWS // GROUPS


def roll(x, shift, axis):
    shift %= x.shape[axis]
    return x if shift == 0 else pltpu.roll(x, shift, axis)


def lane_ids():
    return lax.broadcasted_iota(jnp.int32, (ROWS, LANES), 1)


def pad4(units):
    return list(units) + [jnp.zeros_like(units[0])] * (GROUPS - len(units))


def exchange4(x):
    group = lane_ids() // SPAN
    low, even = group < 2, group % 2 == 0
    a = [jnp.where(low, x[u], roll(x[u + 2], 64, 1)) for u in range(2)]
    b = [jnp.where(low, roll(x[u], 64, 1), x[u + 2]) for u in range(2)]
    out = []
    for first, second in (a, b):
        out.append(jnp.where(even, first, roll(second, SPAN, 1)))
        out.append(jnp.where(even, roll(first, -SPAN, 1), second))
    return out


def windows(units, own):
    halo, phases, length = (SPAN - own) // 2, SPAN // own, units[0].shape[1]
    for phase in range(phases):
        moved = pad4([roll(u, halo - own * phase, 1) for u in units])
        for tile in range(length // LANES):
            parts = exchange4([m[:, tile * LANES : (tile + 1) * LANES] for m in moved])
            for q, part in enumerate(parts):
                yield (tile * GROUPS + q) * phases + phase, part


class Sizes:
    def __init__(self, mesh_shape, members_here, variables, lon, obs_here):
        self.mem, self.lat, self.win = (mesh_shape[a] for a in ("mem", "lat", "win"))
        self.devices = self.mem * self.lat * self.win
        self.members_here, self.variables, self.lon = members_here, variables, lon
        self.members = members_here * self.mem
        self.vars_here = variables // self.win
        self.own = lon // self.devices
        self.halo = (SPAN - self.own) // 2
        self.tiles = self.lat // 2
        self.pairs = self.win // 2
        self.obs_rows = obs_here // self.win // LANES
        self.ens_regs = pl.cdiv(members_here * self.vars_here, GROUPS)
        self.dif_regs = pl.cdiv(self.vars_here, GROUPS)
        self.dif_at = ROWS * self.ens_regs
        self.wts_at = self.dif_at + ROWS * self.dif_regs
        self.obs_at = self.wts_at + HALF
        self.chunk = self.obs_at + 4 * self.obs_rows
        self.back = PAIR + ROWS
        assert lon // self.mem == LANES and members_here * SPAN <= LANES // 2 and members_here * self.own <= SPAN
        assert self.chunk % HALF == 0
        assert self.halo >= 2 * DIFF * ITERS
        assert self.lat % 2 == 0 and self.win % 2 == 0 and variables % self.win == 0
        assert SPAN % self.own == 0 and variables * self.own <= LANES
        assert obs_here % (self.win * LANES) == 0

    def slot(self, d):
        mem, rest = divmod(d, self.lat * self.win)
        lat, win = divmod(rest, self.win)
        return (lat * self.mem + mem) * self.win + win


def turn(x):
    pair = lax.broadcasted_iota(jnp.int32, (ROWS, LANES), 0) // PAIR
    group = lane_ids() // SPAN
    x = jnp.where(pair // 2 == group // 2, x, roll(roll(x, LANES // 2, 1), HALF, 0))
    up, down = roll(roll(x, -PAIR, 0), SPAN, 1), roll(roll(x, PAIR, 0), -SPAN, 1)
    return jnp.where(pair % 2 == group % 2, x, jnp.where(pair % 2 == 0, up, down))


def pack_kernel(z, steps, *refs):
    sources, (out, coup, error), scratch, sems = refs[:9], refs[9:12], refs[12:21], refs[21]
    coupling_in, error_in, dif, ens, cell, window, value, weight, wts = scratch
    k = lax.axis_index("win")
    mine = pl.ds(k * z.vars_here, z.vars_here)
    copies = []
    for n, (source, target) in enumerate(zip(sources, scratch)):
        source = source.at[mine] if target is dif else source.at[:, mine] if target is ens else source
        copies.append(pltpu.make_async_copy(source, target, sems.at[n]))
        copies[-1].start()
    copies[0].wait()
    copies[1].wait()
    for v in range(z.variables):
        error[v] = jnp.broadcast_to(error_in[:, v : v + 1], (ROWS, LANES))
        for w in range(z.variables):
            coup[v, w] = jnp.broadcast_to(coupling_in[v : v + 1, w : w + 1], (ROWS, LANES))
    copies[2].wait()
    per_block = LANES // z.own
    count = jnp.full((ROWS, LANES), steps[0], jnp.int32).astype(jnp.float32)
    spare = lane_ids() % SPAN == 0
    for reg in range(z.dif_regs):
        mine = range(reg * GROUPS, min(z.vars_here, (reg + 1) * GROUPS))
        for d, part in windows([dif[v] for v in mine], z.own):
            part = jnp.where(spare, count, part)
            for block in range(z.mem):
                at = z.slot(block * per_block + d) * z.chunk + z.dif_at + reg * ROWS
                out[at : at + ROWS, :] = part
    for copy in copies[3:8]:
        copy.wait()
    n = z.obs_rows
    tables = []
    for ref in (cell, window, value, weight):
        rows = ref[0:n, :]
        for other in range(1, z.win):
            rows = jnp.where(k == other, ref[other * n : (other + 1) * n, :], rows)
        tables.append(rows.astype(jnp.float32))
    units = [ens[m, v] for m in range(z.members_here) for v in range(z.vars_here)]
    for reg in range(z.ens_regs):
        for d, part in windows(units[reg * GROUPS : (reg + 1) * GROUPS], z.own):
            at = z.slot(d) * z.chunk + reg * ROWS
            out[at : at + ROWS, :] = part
    copies[8].wait()
    low = lane_ids() < LANES // 2
    for d, part in windows([wts[0, m] for m in range(z.members_here)], z.own):
        at = z.slot(d) * z.chunk + z.wts_at
        out[at : at + HALF, :] = jnp.where(low, part, roll(roll(part, LANES // 2, 1), HALF, 0))[:HALF]
    for a, rows in enumerate(tables):
        for d in range(z.devices):
            at = d * z.chunk + z.obs_at + a * n
            out[at : at + n, :] = rows


def spread4(first, second):
    group = lane_ids() // SPAN
    low, even = group < 2, group % 2 == 0
    a = jnp.where(even, first, roll(second, SPAN, 1))
    b = jnp.where(even, roll(first, -SPAN, 1), second)
    a2, b2 = roll(a, 64, 1), roll(b, 64, 1)
    return [jnp.where(low, a, a2), jnp.where(low, b, b2), jnp.where(low, a2, a), jnp.where(low, b2, b)]


def place(pieces, width):
    block = lane_ids() // width
    out = None
    for x, source, target in pieces:
        moved = roll(x, target - source, 1)
        out = moved if out is None else jnp.where(block == target // width, moved, out)
    return out


def split(x):
    high = x.astype(jnp.bfloat16).astype(jnp.float32)
    return high, x - high


def descend_kernel(z, scale, coup, error_weight, recv, out, ens, dif, own, slope, bias):
    i, j, k = (lax.axis_index(a) for a in ("mem", "lat", "win"))
    d = (i * z.lat + j) * z.win + k
    start = lax.rem(d * z.own - z.halo + z.lon, z.lon)
    left = lax.div(start, LANES)
    right = lax.div(lax.rem(start + SPAN - 1, z.lon), LANES)
    lanes = lane_ids()
    sub = lax.broadcasted_iota(jnp.int32, (ROWS, LANES), 0)
    group = lanes // SPAN
    upper = group % 2 == 0
    in_left = start + lanes % SPAN < (left + 1) * LANES
    T, NV, M = z.tiles, z.variables, z.members

    def source(mem, lat, win):
        return (mem * z.lat + lat) * z.win + win

    def take(mem, lat, win, at, rows):
        first = ((lat * z.mem + mem) * z.win + win) * z.chunk
        return recv[pl.ds((first if isinstance(first, int) else pl.multiple_of(first, HALF)) + at, rows), :]

    for mem in range(z.mem):
        for win in range(z.win):
            for reg in range(z.ens_regs):
                for t in range(T):
                    got = spread4(*(take(mem, h * T + t, win, reg * ROWS, ROWS) for h in range(2)))
                    for u, part in enumerate(got):
                        unit = reg * GROUPS + u
                        if unit < z.members_here * z.vars_here:
                            m = mem * z.members_here + unit // z.vars_here
                            v = win * z.vars_here + unit % z.vars_here
                            ens[m, v, t] = part
    for win in range(z.win):
        for reg in range(z.dif_regs):
            at = z.dif_at + reg * ROWS
            for t in range(T):
                both = [
                    jnp.where(in_left, take(left, h * T + t, win, at, ROWS), take(right, h * T + t, win, at, ROWS))
                    for h in range(2)
                ]
                for u, part in enumerate(spread4(*both)):
                    if reg * GROUPS + u < z.vars_here:
                        dif[win * z.vars_here + reg * GROUPS + u, t] = jnp.where(lanes % SPAN == 0, 0.0, part)

    def weights_of(mem, lat, win):
        x = take(mem, lat, win, z.wts_at, HALF)
        return jnp.concatenate([x, roll(x, LANES // 2, 1)], 0)

    control = [[[None] * T for _ in range(z.pairs)] for _ in range(M)]
    for mem in range(z.mem):
        for p in range(z.pairs):
            for t in range(T):
                quarter = [weights_of(mem, h * T + t, 2 * p + w) for w in range(2) for h in range(2)]
                for unit in range(z.members_here):
                    control[mem * z.members_here + unit][p][t] = place([(x, SPAN * unit, SPAN * g) for g, x in enumerate(quarter)], SPAN)
    steps = [jnp.broadcast_to(take(0, 0, win, z.dif_at, 1)[:, :1], (ROWS, LANES)) for win in range(z.win)]
    counts = [jnp.where(group < 2, steps[2 * p], steps[2 * p + 1]).astype(jnp.int32) for p in range(z.pairs)]

    bf16 = jnp.bfloat16
    id_type = bf16 if z.win * NV * ROWS <= 256 else jnp.float32
    row_id = lax.broadcasted_iota(jnp.int32, (z.win * NV * ROWS, LANES), 0).astype(jnp.float32).astype(id_type)
    lane_id = lax.broadcasted_iota(jnp.int32, (SPAN, LANES), 0).astype(jnp.float32).astype(bf16)
    one, none = jnp.ones((), bf16), jnp.zeros((), bf16)
    n = z.obs_rows

    def column(x, like):
        return jnp.broadcast_to(x, like.shape).astype(like.dtype)

    for lat in range(z.lat):
        hot, parts = [], []
        for side, block in enumerate((left, right)):
            for win in range(z.win):
                where, time, value, weight = (take(block, lat, win, z.obs_at + a * n, n) for a in range(4))
                where = where.astype(jnp.int32)
                weighted = weight * value
                lane = block * LANES + where % LANES - start
                lane = jnp.where(lane < 0, lane + z.lon, lane)
                inside = lane < SPAN
                if side == 1:
                    inside &= left != right
                lane = jnp.where(inside, lane, -1).astype(jnp.float32)
                row = time * (NV * ROWS) + (where // LANES).astype(jnp.float32)
                values = [x for pair in zip(split(weight), split(weighted)) for x in pair]
                for x in range(n):
                    at = slice(x, x + 1)
                    hit = column(lane[at], lane_id) == lane_id
                    hot.append(jnp.where(column(row[at], row_id) == row_id, one.astype(id_type), none.astype(id_type)).astype(bf16))
                    parts.append(jnp.concatenate([jnp.where(hit, column(y[at], lane_id), none) for y in values], 0))
        total = lax.dot_general(
            jnp.concatenate(hot, 1),
            jnp.concatenate(parts, 1),
            (((1,), (1,)), ((), ())),
            preferred_element_type=jnp.float32,
        )
        h, t = divmod(lat, T)
        for p in range(z.pairs):
            for v in range(NV):
                sums = []
                for w in range(2):
                    at = ((2 * p + w) * NV + v) * ROWS
                    x = total[at : at + ROWS, :]
                    sums.append(x + roll(x, 2 * SPAN, 1))
                both = jnp.where(group < 2, sums[0], sums[1])
                x, y = (both, roll(both, -SPAN, 1)) if h == 0 else (roll(both, SPAN, 1), both)
                if h == 0:
                    slope[p, v, t], bias[p, v, t] = x, y
                else:
                    slope[p, v, t] = jnp.where(upper, slope[p, v, t], x)
                    bias[p, v, t] = jnp.where(upper, bias[p, v, t], y)

    first, last = sub == 0, sub == ROWS - 1

    def beside(x):
        down = [roll(a, 1, 0) for a in x]
        up = [roll(a, -1, 0) for a in x]
        before_first = jnp.where(upper, 0.0, roll(down[T - 1], SPAN, 1))
        after_last = jnp.where(upper, roll(up[0], -SPAN, 1), 0.0)
        return [
            jnp.where(first, down[t - 1] if t else before_first, down[t])
            + jnp.where(last, up[t + 1] if t < T - 1 else after_last, up[t])
            for t in range(T)
        ]

    def smooth(x):
        for _ in range(DIFF):
            x = [
                (1.0 - 4.0 * KAPPA) * a + KAPPA * (rows + roll(a, 1, 1) + roll(a, -1, 1))
                for a, rows in zip(x, beside(x))
            ]
        return x

    def weigh(terms):
        total = None
        for factor, x in terms:
            total = factor * x if total is None else total + factor * x
        return total

    for v in range(NV):
        for t in range(T):
            own[v, t] = 1.0 - 2.0 * dif[v, t] + coup[v, v]

    def repeat(step, state, p):
        def section(index, flat):
            moved = step([list(flat[v * T : (v + 1) * T]) for v in range(NV)])
            on = index < counts[p]
            return tuple(jnp.where(on, x, y) for x, y in zip((x for v in moved for x in v), flat))

        flat = lax.fori_loop(0, most[p], section, tuple(x for v in state for x in v))
        return [list(flat[v * T : (v + 1) * T]) for v in range(NV)]

    def forward(u):
        moved = []
        for v in range(NV):
            near = beside(u[v])
            moved.append([
                own[v, t] * u[v][t] + dif[v, t] * near[t] + weigh((coup[v, w], u[w][t]) for w in range(NV) if w != v)
                for t in range(T)
            ])
        return moved

    def backward(u):
        moved = []
        for v in range(NV):
            near = beside([dif[v, t] * u[v][t] for t in range(T)])
            moved.append([
                own[v, t] * u[v][t] + near[t] + weigh((coup[w, v], u[w][t]) for w in range(NV) if w != v) for t in range(T)
            ])
        return moved

    most = [jnp.max(c) for c in counts]
    later = group >= 2
    zero = jnp.zeros((ROWS, LANES), jnp.float32)
    for _ in range(ITERS):
        increment, ends = [], []
        smoothed = [[smooth(control[m][p]) for p in range(z.pairs)] for m in range(M)]
        for p in range(z.pairs):
            increment.append(
                [[weigh((ens[m, v, t], smoothed[m][p][t]) for m in range(M)) * scale for t in range(T)] for v in range(NV)]
            )
            ends.append(repeat(forward, increment[p], p))
        misfit = []
        for p in range(z.pairs):
            misfit.append([])
            for v in range(NV):
                misfit[p].append([])
                for t in range(T):
                    before = roll(ends[p][v][t], 64, 1)
                    if p:
                        before = jnp.where(later, before, roll(ends[p - 1][v][t], 64, 1))
                    x = error_weight[v] * (before - increment[p][v][t])
                    misfit[p][v].append(x if p else jnp.where(later, x, 0.0))
        members_back = [[] for _ in range(M)]
        for p in range(z.pairs):
            forcing = []
            for v in range(NV):
                forcing.append([])
                for t in range(T):
                    after = roll(misfit[p + 1][v][t], 64, 1) if p + 1 < z.pairs else zero
                    after = jnp.where(later, after, roll(misfit[p][v][t], 64, 1))
                    forcing[v].append(slope[p, v, t] * ends[p][v][t] - bias[p, v, t] + after)
            adjoint = repeat(backward, forcing, p)
            gradient = [[adjoint[v][t] - misfit[p][v][t] for t in range(T)] for v in range(NV)]
            for m in range(M):
                members_back[m].append(
                    [weigh((ens[m, v, t], gradient[v][t]) for v in range(NV)) * scale for t in range(T)]
                )
        for m in range(M):
            for p in range(z.pairs):
                pulled = smooth(members_back[m][p])
                control[m][p] = [c - DESCENT * (c + x) for c, x in zip(control[m][p], pulled)]

    for lat in range(z.lat):
        h, t = divmod(lat, T)
        for win in range(z.win):
            p, w = divmod(win, 2)
            lane = SPAN * (2 * w + h) + z.halo
            grown = place([(increment[p][v][t], lane, z.own * v) for v in range(NV)], z.own)
            for first_mem in range(0, z.mem, GROUPS):
                mems = range(first_mem, min(z.mem, first_mem + GROUPS))
                x = place(
                    [
                        (control[mem * z.members_here + m][p][t], lane, SPAN * (mem - first_mem) + z.own * m)
                        for mem in mems
                        for m in range(z.members_here)
                    ],
                    z.own,
                )
                x = turn(x)
                for mem in mems:
                    to, at = source(mem, lat, win) * z.back, PAIR * (mem - first_mem)
                    out[to : to + PAIR, :] = x[at : at + PAIR]
                    out[to + PAIR : to + z.back, :] = grown


def unpack_kernel(z, recv, control, increment):
    per_tile = LANES // z.own
    for tile in range(z.lon // LANES):
        pieces = []
        for batch in range(0, per_tile, GROUPS):
            x = turn(jnp.concatenate(
                [recv[d * z.back : d * z.back + PAIR, :] for d in range(tile * per_tile + batch, tile * per_tile + batch + GROUPS)], 0
            ))
            pieces += [(x, SPAN * g, z.own * (batch + g)) for g in range(GROUPS)]
        for m in range(z.members_here):
            control[0, m, :, tile * LANES : (tile + 1) * LANES] = place(
                [(x, source + z.own * m, target) for x, source, target in pieces], z.own
            )
    first = lax.axis_index("mem") * per_tile
    got = [recv[pl.ds(pl.multiple_of((first + q) * z.back, PAIR) + PAIR, ROWS), :] for q in range(per_tile)]
    for v in range(z.variables):
        increment[0, v] = place([(x, z.own * v, z.own * q) for q, x in enumerate(got)], z.own)


def in_hbm(*arrays):
    return [pltpu.with_memory_space_constraint(x, pltpu.HBM) for x in arrays]


def solution(mesh):
    smem = pl.BlockSpec(memory_space=pltpu.SMEM)
    vmem = pl.BlockSpec(memory_space=pltpu.VMEM)
    hbm = pl.BlockSpec(memory_space=pltpu.HBM)
    f32 = jnp.float32

    def local(ensemble, weights, diffusivity, coupling, tl_steps, obs_cell, obs_window, obs_value, obs_weight, error_weight):
        z = Sizes(mesh.shape, ensemble.shape[0], ensemble.shape[1], ensemble.shape[3], obs_cell.shape[0])
        scale = 1.0 / math.sqrt(z.members - 1)
        tables = [x.reshape(-1, LANES) for x in (obs_cell, obs_window, obs_value, obs_weight)]
        params = pltpu.CompilerParams(vmem_limit_bytes=24 << 20)
        reg = (ROWS, LANES)
        field = pltpu.VMEM((z.pairs, z.variables, z.tiles, *reg), f32)
        still = pltpu.VMEM((z.variables, z.tiles, *reg), f32)

        def exchange(x, rows, axes):
            step = math.gcd(rows, ROWS)
            split = x.reshape(z.devices, rows // step, step, LANES)
            return lax.all_to_all(split, axes, 0, 0).reshape(x.shape)

        sent, coup, error = pl.pallas_call(
            lambda *refs: pack_kernel(z, *refs),
            out_shape=(
                jax.ShapeDtypeStruct((z.devices * z.chunk, LANES), f32),
                jax.ShapeDtypeStruct((z.variables, z.variables, *reg), f32),
                jax.ShapeDtypeStruct((z.variables, *reg), f32),
            ),
            in_specs=[smem] + [hbm] * 9,
            out_specs=(vmem, vmem, vmem),
            scratch_shapes=[
                pltpu.VMEM(coupling.shape, f32),
                pltpu.VMEM((1, z.variables), f32),
                pltpu.VMEM((z.vars_here, *reg), f32),
                pltpu.VMEM((z.members_here, z.vars_here, ROWS, z.lon), f32),
                *(pltpu.VMEM(x.shape, x.dtype) for x in tables),
                pltpu.VMEM(weights.shape, f32),
                pltpu.SemaphoreType.DMA((9,)),
            ],
            compiler_params=params,
            name="pack",
        )(tl_steps, *in_hbm(coupling, error_weight.reshape(1, -1), diffusivity, ensemble, *tables, weights))
        back = pl.pallas_call(
            lambda *refs: descend_kernel(z, scale, *refs),
            out_shape=jax.ShapeDtypeStruct((z.devices * z.back, LANES), f32),
            in_specs=[vmem, vmem, vmem],
            out_specs=vmem,
            scratch_shapes=[
                pltpu.VMEM((z.members, z.variables, z.tiles, *reg), f32),
                still,
                still,
                field,
                field,
            ],
            compiler_params=params,
            name="descend",
        )(coup, error, exchange(sent, z.chunk, ("lat", "mem", "win")))
        home = exchange(back, z.back, ("mem", "lat", "win"))
        return pl.pallas_call(
            lambda *refs: unpack_kernel(z, *refs),
            out_shape=(
                jax.ShapeDtypeStruct(weights.shape, f32),
                jax.ShapeDtypeStruct((1, z.variables, ROWS, LANES), f32),
            ),
            in_specs=[vmem],
            out_specs=(vmem, vmem),
            compiler_params=params,
            name="unpack",
        )(home)

    return jax.shard_map(
        local,
        mesh=mesh,
        in_specs=(
            P("mem", None, "lat", None),
            P("win", "mem", "lat", None),
            P(None, "lat", "mem"),
            P(),
            P("win"),
            P(("mem", "lat")),
            P(("mem", "lat")),
            P(("mem", "lat")),
            P(("mem", "lat")),
            P(),
        ),
        out_specs=(P("win", "mem", "lat", None), P("win", None, "lat", "mem")),
        check_vma=False,
    )
```
